256 devices in a mesh: rows: 8 (over x, z_hi), specs: 32 (over y, z_lo, core).
Axes of the slice: x: 4, y: 4, z: 8 (z_hi: 2, z_lo: 4; z = z_hi * 4 + z_lo), core: 2. Of those that a mesh axis runs over, the one named last changes fastest.
Arguments:
- center: float32 [64, 512, 64], P('rows'), may hold values from -6 to 6
- radius: float32 [64, 512, 64], P('rows'), may hold values from 0.01 to 0.2
- conv_weight: float32 [3, 3, 64, 64], replicated, may hold values from -0.25 to 0.25
- conv_bias: float32 [64], replicated, may hold values from -3 to 3
- split_status: int32 [64, 512, 64], P('rows'), may hold values from 0 to 2
- out_coeffs: bfloat16 [256, 64, 512, 64], P('specs', 'rows'), may hold values from -6 to 6
- spec_ids: int32 [256], P('specs'), may hold values from 0 to 4095
- spec_offsets: float32 [4096], replicated, may hold values from -5 to 5
Outputs:
- input_coeffs: bfloat16 [256, 64, 512, 64], P('specs', 'rows')
- bounds: float32 [256], P('specs')
The draws below stay inside these ranges and needn't reach their ends.
All inputs are finite; a program needn't handle non-finite values.
Results may differ from the reference program's by a relative error of at most 0.0052.
Values may be sent and summed in bfloat16 or wider, within the bound.
No kernel may reach another device: no remote copies, remote signals or barrier semaphores. Data moves between devices by JAX's collectives and lax.ppermute only.
A program may use at most 128 MiB of HBM per device.

```python
import math
import jax
import jax.numpy as jnp
from jax import lax

C = 64
W = 512
SPEC_TABLE = 4096
H = 64
SPECS = 256


def set_ends(values, stream_key, least, top_value):
    longest = values.shape.index(max(values.shape))
    spots = []
    for shift in (0, 1):
        where = [jax.random.randint(jax.random.fold_in(stream_key, axis), (), 0, length) for axis, length in enumerate(values.shape)]
        where[longest] = (where[longest] + shift) % values.shape[longest]
        spots.append(tuple(where))
    return values.at[spots[0]].set(least).at[spots[1]].set(top_value)


def level_of(key, extent, cuts, smallest, top_value):
    gain = 1.0
    for axis_at, parts in cuts:
        heights = jax.random.uniform(jax.random.fold_in(jax.random.fold_in(key, 6), axis_at), (parts,), jnp.float32, smallest / len(cuts), top_value / len(cuts))
        gain = gain * jnp.repeat(jnp.exp(heights), extent[axis_at] // parts).reshape((-1,) + (1,) * (len(extent) - 1 - axis_at))
    return gain


def noise(stream_key, shape, scale, most, split=(), dtype=jnp.bfloat16):
    loudness = level_of(stream_key, shape, split, -0.22, 0.18) if split else 1.0
    drawn = jax.random.normal(stream_key, shape, jnp.float32) * scale * loudness
    return jnp.minimum(jnp.maximum(drawn, -most), most).astype(dtype)


def setup_inputs(seed: int = 0) -> dict:
    streams_of = jax.random.split(jax.random.key(seed), 9)
    return {
        "center": noise(streams_of[0], (H, W, C), 1.0, 6.0, ((0, 8),), jnp.float32),
        "radius": jnp.clip(jnp.exp(math.log(0.2) - 2.9957323 * jax.random.uniform(streams_of[1], (H, W, C), jnp.float32) ** level_of(streams_of[1], (H, W, C), ((0, 8),), -0.2, 0.2)), 0.01, 0.2),
        "conv_weight": noise(streams_of[2], (3, 3, C, C), (9 * C) ** -0.5, 0.25, (), jnp.float32),
        "conv_bias": noise(streams_of[3], (C,), 0.5, 3.0, (), jnp.float32),
        "split_status": set_ends(jax.random.randint(streams_of[4], (H, W, C), 0, 3), jax.random.fold_in(streams_of[4], 1), 0, 2).astype(jnp.int32),
        "out_coeffs": noise(streams_of[5], (SPECS, H, W, C), 1.0, 6.0, ((0, 32), (1, 8))),
        "spec_ids": set_ends(jax.random.randint(streams_of[6], (SPECS,), 0, SPEC_TABLE), jax.random.fold_in(streams_of[6], 1), 0, SPEC_TABLE - 1).astype(jnp.int32),
        "spec_offsets": noise(streams_of[7], (SPEC_TABLE,), 1.0, 5.0, (), jnp.float32),
    }


def shifted_sum(padded, kernel):
    result = jnp.zeros((H, W, C), jnp.float32)
    for i in range(3):
        for j in range(3):
            result = result + jnp.einsum("hwc,cd->hwd", padded[i:i + H, j:j + W], kernel[i, j], precision=lax.Precision.HIGHEST)
    return result


def reference(center, radius, conv_weight, conv_bias, split_status, out_coeffs, spec_ids, spec_offsets):
    edges = ((1, 1), (1, 1), (0, 0))
    center_out = conv_bias + shifted_sum(jnp.pad(center, edges), conv_weight)
    radius_out = shifted_sum(jnp.pad(radius, edges), jnp.abs(conv_weight))
    upper_end = center_out + radius_out
    lower_end = center_out - radius_out
    spread = 2.0 * radius_out
    relaxed = jnp.minimum(jnp.maximum(upper_end, 0.0), spread) / spread
    slopes = jnp.where(split_status == 2, relaxed, jnp.where(split_status == 1, 1.0, 0.0)).astype(jnp.bfloat16)
    intercepts = jnp.where(split_status == 2, -relaxed * jnp.minimum(lower_end, 0.0), 0.0).astype(jnp.bfloat16)
    weight_low = conv_weight.astype(jnp.bfloat16).astype(jnp.float32)

    def one_spec(coeffs):
        coeff_full = coeffs.astype(jnp.float32)
        pre_coeffs = (coeff_full * slopes.astype(jnp.float32)).astype(jnp.bfloat16)
        pre_full = pre_coeffs.astype(jnp.float32)
        offset_sum = jnp.sum(jnp.minimum(coeff_full, 0.0) * intercepts.astype(jnp.float32)) + jnp.sum(pre_full * conv_bias)
        padded = jnp.pad(pre_full, edges)
        input_coeffs = jnp.zeros((H, W, C), jnp.float32)
        for i in range(3):
            for j in range(3):
                input_coeffs = input_coeffs + jnp.einsum("hwd,cd->hwc", padded[2 - i:2 - i + H, 2 - j:2 - j + W], weight_low[i, j])
        summed = jnp.sum(input_coeffs * center - jnp.abs(input_coeffs) * radius) + offset_sum
        return input_coeffs.astype(jnp.bfloat16), summed / (H * W)

    input_coeffs, bounds = lax.map(one_spec, out_coeffs)
    return input_coeffs, bounds + spec_offsets[spec_ids]
```

```python
import functools

import jax
import jax.numpy as jnp
from jax import lax
from jax.experimental import pallas as pl
from jax.experimental.pallas import tpu as pltpu
from jax.sharding import PartitionSpec as P

F32, BF16 = (jnp.float32, jnp.bfloat16)
SHARE = 8
UNITS = 7


def spread_columns(stack, columns):
    size = stack.shape[0] // 3
    where = lax.broadcasted_iota(jnp.int32, (size, columns), 1)
    right = pltpu.roll(stack[:size], 1, 1)
    left = pltpu.roll(stack[2 * size :], columns - 1, 1)
    right = jnp.where(where == 0, 0.0, right)
    left = jnp.where(where == columns - 1, 0.0, left)
    return right + stack[size : 2 * size] + left


def mul(a, b):
    return jnp.dot(a, b, preferred_element_type=F32)


def high_low(value):
    high = value.astype(BF16)
    return high, (value - high.astype(F32)).astype(BF16)


def send_kernel(
    where_ref,
    center_ref,
    radius_ref,
    status_ref,
    coeff_ref,
    out_ref,
    last_ref,
    first_ref,
    sems,
):
    rows = coeff_ref.shape[1]
    copies = [
        pltpu.make_async_copy(coeff_ref.at[:, rows - 1], last_ref, sems.at[0]),
        pltpu.make_async_copy(coeff_ref.at[:, 0], first_ref, sems.at[1]),
    ]
    for copy in copies:
        copy.start()
    high, low = high_low(center_ref[...])
    out_ref[0:2] = high
    out_ref[2:4] = low
    out_ref[4:6] = radius_ref[...].astype(BF16)
    out_ref[6:7] = status_ref[...].astype(F32).astype(BF16)
    for copy in copies:
        copy.wait()


def send_pass(where, center, radius, status, coeffs):
    specs, rows, channels, columns = coeffs.shape
    part = channels * 2 // SHARE
    box = pl.BlockSpec((2, part, columns), lambda g, w: (w[0], w[1], 0))
    edge = jax.ShapeDtypeStruct((specs, channels, columns), BF16)
    return pl.pallas_call(
        send_kernel,
        out_shape=(jax.ShapeDtypeStruct((UNITS, part, columns), BF16), edge, edge),
        grid_spec=pltpu.PrefetchScalarGridSpec(
            num_scalar_prefetch=1,
            grid=(1,),
            in_specs=[
                box,
                box,
                pl.BlockSpec((1, part, columns), lambda g, w: (w[2], w[1], 0)),
                pl.BlockSpec(memory_space=pl.ANY),
            ],
            out_specs=(
                pl.BlockSpec((UNITS, part, columns), lambda g, w: (0, 0, 0)),
                pl.BlockSpec(memory_space=pl.ANY),
                pl.BlockSpec(memory_space=pl.ANY),
            ),
            scratch_shapes=[pltpu.SemaphoreType.DMA((2,))],
        ),
    )(where, center, radius, status, coeffs)


def main_kernel(
    halo_ref,
    center_ref,
    radius_ref,
    status_ref,
    forward_ref,
    absolute_ref,
    backward_ref,
    bias_ref,
    coeff_ref,
    out_ref,
    edge_ref,
    slope_edge_ref,
    total_ref,
    ch_ref,
    cl_ref,
    rh_ref,
    rl_ref,
    status_ext_ref,
    slope_ref,
    intercept_ref,
    linear_ref,
    pre_ref,
):
    rows, channels, columns = center_ref.shape
    c = channels
    part = halo_ref.shape[2]

    @pl.when(pl.program_id(0) == 0)
    def _():
        for side, base in ((0, 0), (1, rows + 2)):
            for y in range(c // part):
                piece = halo_ref.at[2 * y + side]
                for k in range(2):
                    at = pl.ds((base + k) * c + y * part, part)
                    ch_ref[at, :] = piece[k]
                    cl_ref[at, :] = piece[2 + k]
                    rh_ref[at, :] = piece[4 + k]
                    rl_ref[at, :] = jnp.zeros((part, columns), BF16)
                row = 0 if side == 0 else rows + 1
                status_ext_ref[pl.ds(row * c + y * part, part), :] = piece[6]
        for h in range(rows):
            at = pl.ds((h + 2) * c, c)
            ch_ref[at, :], cl_ref[at, :] = high_low(center_ref[h])
            rh_ref[at, :], rl_ref[at, :] = high_low(radius_ref[h])
            status_ext_ref[pl.ds((h + 1) * c, c), :] = status_ref[h].astype(F32).astype(BF16)
        pre_ref[pl.ds(0, c), :] = jnp.zeros((c, columns), BF16)
        pre_ref[pl.ds((rows + 1) * c, c), :] = jnp.zeros((c, columns), BF16)

        @pl.loop(0, (rows + 2) // 2)
        def _(b):
            at = pl.ds(pl.multiple_of(b * 2 * c, 2 * c), 4 * c)
            here = pl.ds(pl.multiple_of(b * 2 * c, 2 * c), 2 * c)
            six = 6 * c
            fh, fl = (forward_ref[:six, :], forward_ref[six:, :])
            ah, al = (absolute_ref[:six, :], absolute_ref[six:, :])
            low = spread_columns(mul(fh, ch_ref[at, :]) + mul(fh, cl_ref[at, :]), columns)
            linear = low + bias_ref[...]
            center_out = linear + spread_columns(mul(fl, ch_ref[at, :]), columns)
            radius_out = spread_columns(
                mul(ah, rh_ref[at, :]) + mul(ah, rl_ref[at, :]) + mul(al, rh_ref[at, :]), columns
            )
            upper = center_out + radius_out
            lower = center_out - radius_out
            width = 2.0 * radius_out
            relaxed = jnp.minimum(jnp.maximum(upper, 0.0), width) / width
            status = status_ext_ref[here, :].astype(F32)
            open_ = status == 2.0
            slope = jnp.where(open_, relaxed, jnp.where(status == 1.0, 1.0, 0.0))
            slope_ref[here, :] = slope.astype(BF16)
            intercept = jnp.where(open_, -relaxed * jnp.minimum(lower, 0.0), 0.0)
            intercept_ref[here, :] = intercept.astype(BF16)
            linear_ref[here, :] = linear

        slope_edge_ref[0] = slope_ref[pl.ds(0, c), :]
        slope_edge_ref[1] = slope_ref[pl.ds((rows + 1) * c, c), :]

    total = jnp.zeros((8, columns), F32)
    for h in range(rows):
        at = pl.ds((h + 1) * c, c)
        coeff = coeff_ref[0, h]
        wide = coeff.astype(F32)
        pre = (wide * slope_ref[at, :].astype(F32)).astype(BF16)
        pre_ref[at, :] = pre
        terms = (
            jnp.minimum(wide, 0.0) * intercept_ref[at, :].astype(F32)
            + pre.astype(F32) * linear_ref[at, :]
        )
        total = total + jnp.sum(terms.reshape(c // 8, 8, columns), axis=0)

    for b in range(rows // 2):
        at = pl.ds(b * 2 * c, 4 * c)
        value = spread_columns(mul(backward_ref[...], pre_ref[at, :]), columns)
        for r in range(2):
            h = 2 * b + r
            row = value[r * c : (r + 1) * c]
            if h == 0 or h == rows - 1:
                edge_ref[0, 0 if h == 0 else 1] = row
            else:
                terms = jnp.abs(row) * radius_ref[h]
                total = total - jnp.sum(terms.reshape(c // 8, 8, columns), axis=0)
            out_ref[0, h] = row.astype(BF16)
    folded = total[:, :128]
    for k in range(1, columns // 128):
        folded = folded + total[:, k * 128 : (k + 1) * 128]
    total_ref[0] = folded


def main_pass(halo, center, radius, status, forward, absolute, backward, bias, coeffs):
    specs, rows, channels, columns = coeffs.shape
    whole = lambda a: pl.BlockSpec(a.shape, lambda s, n=a.ndim: (0,) * n)
    ext = (rows + 4) * channels
    mid = (rows + 2) * channels
    return pl.pallas_call(
        main_kernel,
        grid=(specs,),
        out_shape=(
            jax.ShapeDtypeStruct(coeffs.shape, BF16),
            jax.ShapeDtypeStruct((specs, 2, channels, columns), F32),
            jax.ShapeDtypeStruct((2, channels, columns), BF16),
            jax.ShapeDtypeStruct((specs, 8, 128), F32),
        ),
        in_specs=[
            whole(a) for a in (halo, center, radius, status, forward, absolute, backward, bias)
        ]
        + [pl.BlockSpec((1, rows, channels, columns), lambda s: (s, 0, 0, 0))],
        out_specs=(
            pl.BlockSpec((1, rows, channels, columns), lambda s: (s, 0, 0, 0)),
            pl.BlockSpec((1, 2, channels, columns), lambda s: (s, 0, 0, 0)),
            pl.BlockSpec((2, channels, columns), lambda s: (0, 0, 0)),
            pl.BlockSpec((1, 8, 128), lambda s: (s, 0, 0)),
        ),
        scratch_shapes=[pltpu.VMEM((ext, columns), BF16)] * 4
        + [
            pltpu.VMEM((mid, columns), BF16),
            pltpu.VMEM((mid, columns), BF16),
            pltpu.VMEM((mid, columns), BF16),
            pltpu.VMEM((mid, columns), F32),
            pltpu.VMEM((mid, columns), BF16),
        ],
        compiler_params=pltpu.CompilerParams(vmem_limit_bytes=48 << 20),
        cost_estimate=pl.CostEstimate(
            flops=20_000_000_000, bytes_accessed=16 << 20, transcendentals=0
        ),
    )(halo, center, radius, status, forward, absolute, backward, bias, coeffs)


def edge_kernel(
    before_ref,
    after_ref,
    slope_ref,
    edge_ref,
    first_ref,
    last_ref,
    weight_ref,
    total_ref,
    _,
    out_ref,
    sum_ref,
    done_ref,
    sems,
):
    specs, channels, columns = before_ref.shape
    rows = out_ref.shape[1]
    for s in range(specs):
        total = jnp.sum(total_ref[s], axis=0, keepdims=True)
        for k, (halo_ref, radius_ref) in enumerate(((before_ref, first_ref), (after_ref, last_ref))):
            pre = (halo_ref[s].astype(F32) * slope_ref[k].astype(F32)).astype(BF16)
            value = edge_ref[s, k] + spread_columns(mul(weight_ref[k], pre), columns)
            done_ref[s, k] = value.astype(BF16)
            pltpu.make_async_copy(
                done_ref.at[s, k], out_ref.at[s, 0 if k == 0 else rows - 1], sems.at[s, k]
            ).start()
            terms = jnp.abs(value) * radius_ref[0]
            terms = jnp.sum(terms.reshape(channels // 8, 8, columns), axis=0)
            folded = terms[:, :128]
            for m in range(1, columns // 128):
                folded = folded + terms[:, m * 128 : (m + 1) * 128]
            total = total - jnp.sum(folded, axis=0, keepdims=True)
        sum_ref[s : s + 1, :] = total
    for s in range(specs):
        for k in range(2):
            pltpu.make_async_copy(
                done_ref.at[s, k], out_ref.at[s, 0 if k == 0 else rows - 1], sems.at[s, k]
            ).wait()


def edge_pass(before, after, slope, edge, radius, weight, total, out):
    specs, rows, channels, columns = out.shape
    whole = lambda a: pl.BlockSpec(a.shape, lambda g, n=a.ndim: (0,) * n)
    return pl.pallas_call(
        edge_kernel,
        grid=(1,),
        out_shape=(
            jax.ShapeDtypeStruct(out.shape, BF16),
            jax.ShapeDtypeStruct((specs, 128), F32),
        ),
        in_specs=[
            whole(before),
            whole(after),
            whole(slope),
            whole(edge),
            pl.BlockSpec((1, channels, columns), lambda g: (0, 0, 0)),
            pl.BlockSpec((1, channels, columns), lambda g: (rows - 1, 0, 0)),
            whole(weight),
            whole(total),
            pl.BlockSpec(memory_space=pl.ANY),
        ],
        out_specs=(
            pl.BlockSpec(memory_space=pl.ANY),
            pl.BlockSpec((specs, 128), lambda g: (0, 0)),
        ),
        scratch_shapes=[
            pltpu.VMEM((specs, 2, channels, columns), BF16),
            pltpu.SemaphoreType.DMA((specs, 2)),
        ],
        input_output_aliases={8: 0},
        compiler_params=pltpu.CompilerParams(vmem_limit_bytes=32 << 20),
        cost_estimate=pl.CostEstimate(
            flops=400_000_000, bytes_accessed=4 << 20, transcendentals=0
        ),
    )(before, after, slope, edge, radius, radius, weight, total, out)


def bands(kernel):
    flat = jnp.transpose(kernel, (1, 2, 0, 3))
    columns, m, rows, k = flat.shape
    flat = flat.reshape(columns, m, rows * k)
    pair = jnp.stack(
        [jnp.pad(flat, ((0, 0), (0, 0), (0, k))), jnp.pad(flat, ((0, 0), (0, 0), (k, 0)))], axis=1
    )
    return pair.reshape(columns * 2 * m, 4 * k)


def split_weight(kernel):
    high = lax.reduce_precision(kernel, 8, 7)
    both = jnp.stack([high, kernel - high]).astype(BF16)
    return jnp.concatenate([bands(both[0]), bands(both[1])], axis=0)


def per_device(
    center, radius, conv_weight, conv_bias, split_status, out_coeffs, spec_ids, spec_offsets
):
    count, groups = (lax.axis_size("rows"), lax.axis_size("specs"))
    rows, columns, channels = center.shape
    center, radius, status = (jnp.swapaxes(a, 1, 2) for a in (center, radius, split_status))
    coeffs = jnp.swapaxes(out_coeffs, 2, 3)

    lanes = groups // SHARE
    me = lax.axis_index("specs")
    core, y = (lax.rem(me, 2), me // (2 * lanes))
    up = core == 0
    where = jnp.stack(
        [jnp.where(up, rows // 2 - 1, 0), y, jnp.where(up, rows - 1, 0)]
    ).astype(jnp.int32)
    box, last, first = send_pass(where, center, radius, status, coeffs)
    moves = []
    for r in range(count):
        for s in range(groups):
            other = r + (1 if s % 2 == 0 else -1)
            if 0 <= other < count:
                moves.append((r * groups + s, other * groups + s))
    box = lax.ppermute(box, ("rows", "specs"), moves)
    before = lax.ppermute(last, "rows", [(i, i + 1) for i in range(count - 1)])
    after = lax.ppermute(first, "rows", [(i + 1, i) for i in range(count - 1)])
    halo = lax.all_gather(
        box,
        "specs",
        axis_index_groups=[
            [(k * lanes + z) * 2 + e for k in range(SHARE // 2) for e in range(2)]
            for z in range(lanes)
        ],
    )

    turned = jnp.swapaxes(conv_weight, 2, 3)
    forward = split_weight(turned)
    absolute = split_weight(jnp.abs(turned))
    low = conv_weight.astype(BF16)
    backward = bands(low[::-1, ::-1])
    ends = jnp.stack(
        [
            low[2, ::-1].reshape(3 * channels, channels),
            low[0, ::-1].reshape(3 * channels, channels),
        ]
    )
    bias = jnp.tile(conv_bias, 2)[:, None]

    out, edge, slope, total = main_pass(
        halo, center, radius, status, forward, absolute, backward, bias, coeffs
    )
    out, partial = edge_pass(before, after, slope, edge, radius, ends, total, out)

    step = 1
    while step < count:
        partial = partial + lax.ppermute(partial, "rows", [(i, i ^ step) for i in range(count)])
        step *= 2
    summed = jnp.sum(partial, axis=1)
    pixels = rows * count * columns
    entries = spec_offsets.shape[0]
    onehot = spec_ids[:, None] == jnp.arange(entries, dtype=jnp.int32)[None, :]
    table_terms = jnp.sum(jnp.where(onehot, spec_offsets[None, :], 0.0), axis=1)
    bounds = summed / pixels + table_terms
    return (jnp.swapaxes(out, 2, 3), bounds)


def solution(mesh):
    in_specs = (
        P("rows", None, None),
        P("rows", None, None),
        P(),
        P(),
        P("rows", None, None),
        P("specs", "rows", None, None),
        P("specs"),
        P(),
    )
    out_specs = (P("specs", "rows", None, None), P("specs"))
    return jax.shard_map(
        per_device, mesh=mesh, in_specs=in_specs, out_specs=out_specs, check_vma=False
    )
```

```python
import functools

import jax
import jax.numpy as jnp
from jax import lax
from jax.experimental import pallas as pl
from jax.experimental.pallas import tpu as pltpu
from jax.sharding import PartitionSpec as P

F32, BF16 = (jnp.float32, jnp.bfloat16)
SHARE = 8
UNITS = 7


def spread_columns(stack, columns):
    size = stack.shape[0] // 3
    where = lax.broadcasted_iota(jnp.int32, (size, columns), 1)
    right = pltpu.roll(stack[:size], 1, 1)
    left = pltpu.roll(stack[2 * size :], columns - 1, 1)
    right = jnp.where(where == 0, 0.0, right)
    left = jnp.where(where == columns - 1, 0.0, left)
    return right + stack[size : 2 * size] + left


def mul(a, b):
    return jnp.dot(a, b, preferred_element_type=F32)


def high_low(value):
    high = value.astype(BF16)
    return high, (value - high.astype(F32)).astype(BF16)


def send_kernel(
    where_ref,
    center_ref,
    radius_ref,
    status_ref,
    coeff_ref,
    out_ref,
    last_ref,
    first_ref,
    held_ref,
    sems,
):
    rows = coeff_ref.shape[1]
    reads = []
    for k, h in enumerate((rows - 1, 0)):
        reads.append(pltpu.make_async_copy(coeff_ref.at[:, h], held_ref.at[k], sems.at[k]))
        reads[k].start()
    high, low = high_low(center_ref[...])
    out_ref[0:2] = high
    out_ref[2:4] = low
    out_ref[4:6] = radius_ref[...].astype(BF16)
    out_ref[6:7] = status_ref[...].astype(F32).astype(BF16)
    writes = []
    for k, ref in enumerate((last_ref, first_ref)):
        reads[k].wait()
        writes.append(pltpu.make_async_copy(held_ref.at[k], ref, sems.at[2 + k]))
        writes[k].start()
    for k in range(2):
        writes[k].wait()


def send_pass(where, center, radius, status, coeffs):
    specs, rows, channels, columns = coeffs.shape
    part = channels * 2 // SHARE
    box = pl.BlockSpec((2, part, columns), lambda g, w: (w[0], w[1], 0))
    edge = jax.ShapeDtypeStruct((specs, channels, columns), BF16)
    return pl.pallas_call(
        send_kernel,
        out_shape=(jax.ShapeDtypeStruct((UNITS, part, columns), BF16), edge, edge),
        grid_spec=pltpu.PrefetchScalarGridSpec(
            num_scalar_prefetch=1,
            grid=(1,),
            in_specs=[
                box,
                box,
                pl.BlockSpec((1, part, columns), lambda g, w: (w[2], w[1], 0)),
                pl.BlockSpec(memory_space=pl.ANY),
            ],
            out_specs=(
                pl.BlockSpec((UNITS, part, columns), lambda g, w: (0, 0, 0)),
                pl.BlockSpec(memory_space=pl.ANY),
                pl.BlockSpec(memory_space=pl.ANY),
            ),
            scratch_shapes=[
                pltpu.VMEM((2, specs, channels, columns), BF16),
                pltpu.SemaphoreType.DMA((4,)),
            ],
        ),
    )(where, center, radius, status, coeffs)


def main_kernel(
    halo_ref,
    center_ref,
    radius_ref,
    status_ref,
    forward_ref,
    absolute_ref,
    backward_ref,
    bias_ref,
    coeff_ref,
    out_ref,
    edge_ref,
    slope_edge_ref,
    total_ref,
    ch_ref,
    cl_ref,
    rh_ref,
    rl_ref,
    status_ext_ref,
    slope_ref,
    intercept_ref,
    linear_ref,
    pre_ref,
):
    rows, channels, columns = center_ref.shape
    c = channels
    part = halo_ref.shape[2]

    @pl.when(pl.program_id(0) == 0)
    def _():
        for side, base in ((0, 0), (1, rows + 2)):
            for y in range(c // part):
                piece = halo_ref.at[2 * y + side]
                for k in range(2):
                    at = pl.ds((base + k) * c + y * part, part)
                    ch_ref[at, :] = piece[k]
                    cl_ref[at, :] = piece[2 + k]
                    rh_ref[at, :] = piece[4 + k]
                    rl_ref[at, :] = jnp.zeros((part, columns), BF16)
                row = 0 if side == 0 else rows + 1
                status_ext_ref[pl.ds(row * c + y * part, part), :] = piece[6]
        for h in range(rows):
            at = pl.ds((h + 2) * c, c)
            ch_ref[at, :], cl_ref[at, :] = high_low(center_ref[h])
            rh_ref[at, :], rl_ref[at, :] = high_low(radius_ref[h])
            status_ext_ref[pl.ds((h + 1) * c, c), :] = status_ref[h].astype(F32).astype(BF16)
        pre_ref[pl.ds(0, c), :] = jnp.zeros((c, columns), BF16)
        pre_ref[pl.ds((rows + 1) * c, c), :] = jnp.zeros((c, columns), BF16)

        @pl.loop(0, (rows + 2) // 2)
        def _(b):
            at = pl.ds(pl.multiple_of(b * 2 * c, 2 * c), 4 * c)
            here = pl.ds(pl.multiple_of(b * 2 * c, 2 * c), 2 * c)
            six = 6 * c
            fh, fl = (forward_ref[:six, :], forward_ref[six:, :])
            ah, al = (absolute_ref[:six, :], absolute_ref[six:, :])
            low = spread_columns(mul(fh, ch_ref[at, :]) + mul(fh, cl_ref[at, :]), columns)
            linear = low + bias_ref[...]
            center_out = linear + spread_columns(mul(fl, ch_ref[at, :]), columns)
            radius_out = spread_columns(
                mul(ah, rh_ref[at, :]) + mul(ah, rl_ref[at, :]) + mul(al, rh_ref[at, :]), columns
            )
            upper = center_out + radius_out
            lower = center_out - radius_out
            width = 2.0 * radius_out
            relaxed = jnp.minimum(jnp.maximum(upper, 0.0), width) / width
            status = status_ext_ref[here, :].astype(F32)
            open_ = status == 2.0
            slope = jnp.where(open_, relaxed, jnp.where(status == 1.0, 1.0, 0.0))
            slope_ref[here, :] = slope.astype(BF16)
            intercept = jnp.where(open_, -relaxed * jnp.minimum(lower, 0.0), 0.0)
            intercept_ref[here, :] = intercept.astype(BF16)
            linear_ref[here, :] = linear

        slope_edge_ref[0] = slope_ref[pl.ds(0, c), :]
        slope_edge_ref[1] = slope_ref[pl.ds((rows + 1) * c, c), :]

    total = jnp.zeros((8, columns), F32)
    for h in range(rows):
        at = pl.ds((h + 1) * c, c)
        coeff = coeff_ref[0, h]
        wide = coeff.astype(F32)
        pre = (wide * slope_ref[at, :].astype(F32)).astype(BF16)
        pre_ref[at, :] = pre
        terms = (
            jnp.minimum(wide, 0.0) * intercept_ref[at, :].astype(F32)
            + pre.astype(F32) * linear_ref[at, :]
        )
        total = total + jnp.sum(terms.reshape(c // 8, 8, columns), axis=0)

    for b in range(rows // 2):
        at = pl.ds(b * 2 * c, 4 * c)
        value = spread_columns(mul(backward_ref[...], pre_ref[at, :]), columns)
        for r in range(2):
            h = 2 * b + r
            row = value[r * c : (r + 1) * c]
            if h == 0 or h == rows - 1:
                edge_ref[0, 0 if h == 0 else 1] = row
            else:
                terms = jnp.abs(row) * radius_ref[h]
                total = total - jnp.sum(terms.reshape(c // 8, 8, columns), axis=0)
            out_ref[0, h] = row.astype(BF16)
    folded = total[:, :128]
    for k in range(1, columns // 128):
        folded = folded + total[:, k * 128 : (k + 1) * 128]
    total_ref[0] = folded


def main_pass(halo, center, radius, status, forward, absolute, backward, bias, coeffs):
    specs, rows, channels, columns = coeffs.shape
    whole = lambda a: pl.BlockSpec(a.shape, lambda s, n=a.ndim: (0,) * n)
    ext = (rows + 4) * channels
    mid = (rows + 2) * channels
    return pl.pallas_call(
        main_kernel,
        grid=(specs,),
        out_shape=(
            jax.ShapeDtypeStruct(coeffs.shape, BF16),
            jax.ShapeDtypeStruct((specs, 2, channels, columns), F32),
            jax.ShapeDtypeStruct((2, channels, columns), BF16),
            jax.ShapeDtypeStruct((specs, 8, 128), F32),
        ),
        in_specs=[
            whole(a) for a in (halo, center, radius, status, forward, absolute, backward, bias)
        ]
        + [pl.BlockSpec((1, rows, channels, columns), lambda s: (s, 0, 0, 0))],
        out_specs=(
            pl.BlockSpec((1, rows, channels, columns), lambda s: (s, 0, 0, 0)),
            pl.BlockSpec((1, 2, channels, columns), lambda s: (s, 0, 0, 0)),
            pl.BlockSpec((2, channels, columns), lambda s: (0, 0, 0)),
            pl.BlockSpec((1, 8, 128), lambda s: (s, 0, 0)),
        ),
        scratch_shapes=[pltpu.VMEM((ext, columns), BF16)] * 4
        + [
            pltpu.VMEM((mid, columns), BF16),
            pltpu.VMEM((mid, columns), BF16),
            pltpu.VMEM((mid, columns), BF16),
            pltpu.VMEM((mid, columns), F32),
            pltpu.VMEM((mid, columns), BF16),
        ],
        compiler_params=pltpu.CompilerParams(vmem_limit_bytes=48 << 20),
        cost_estimate=pl.CostEstimate(
            flops=20_000_000_000, bytes_accessed=16 << 20, transcendentals=0
        ),
    )(halo, center, radius, status, forward, absolute, backward, bias, coeffs)


def edge_kernel(
    before_ref,
    after_ref,
    slope_ref,
    edge_ref,
    first_ref,
    last_ref,
    weight_ref,
    total_ref,
    _,
    out_ref,
    sum_ref,
    done_ref,
    sems,
):
    specs, channels, columns = before_ref.shape
    rows = out_ref.shape[1]
    for s in range(specs):
        total = jnp.sum(total_ref[s], axis=0, keepdims=True)
        for k, (halo_ref, radius_ref) in enumerate(((before_ref, first_ref), (after_ref, last_ref))):
            pre = (halo_ref[s].astype(F32) * slope_ref[k].astype(F32)).astype(BF16)
            value = edge_ref[s, k] + spread_columns(mul(weight_ref[k], pre), columns)
            done_ref[s, k] = value.astype(BF16)
            pltpu.make_async_copy(
                done_ref.at[s, k], out_ref.at[s, 0 if k == 0 else rows - 1], sems.at[s, k]
            ).start()
            terms = jnp.abs(value) * radius_ref[0]
            terms = jnp.sum(terms.reshape(channels // 8, 8, columns), axis=0)
            folded = terms[:, :128]
            for m in range(1, columns // 128):
                folded = folded + terms[:, m * 128 : (m + 1) * 128]
            total = total - jnp.sum(folded, axis=0, keepdims=True)
        sum_ref[s : s + 1, :] = total
    for s in range(specs):
        for k in range(2):
            pltpu.make_async_copy(
                done_ref.at[s, k], out_ref.at[s, 0 if k == 0 else rows - 1], sems.at[s, k]
            ).wait()


def edge_pass(before, after, slope, edge, radius, weight, total, out):
    specs, rows, channels, columns = out.shape
    whole = lambda a: pl.BlockSpec(a.shape, lambda g, n=a.ndim: (0,) * n)
    return pl.pallas_call(
        edge_kernel,
        grid=(1,),
        out_shape=(
            jax.ShapeDtypeStruct(out.shape, BF16),
            jax.ShapeDtypeStruct((specs, 128), F32),
        ),
        in_specs=[
            whole(before),
            whole(after),
            whole(slope),
            whole(edge),
            pl.BlockSpec((1, channels, columns), lambda g: (0, 0, 0)),
            pl.BlockSpec((1, channels, columns), lambda g: (rows - 1, 0, 0)),
            whole(weight),
            whole(total),
            pl.BlockSpec(memory_space=pl.ANY),
        ],
        out_specs=(
            pl.BlockSpec(memory_space=pl.ANY),
            pl.BlockSpec((specs, 128), lambda g: (0, 0)),
        ),
        scratch_shapes=[
            pltpu.VMEM((specs, 2, channels, columns), BF16),
            pltpu.SemaphoreType.DMA((specs, 2)),
        ],
        input_output_aliases={8: 0},
        compiler_params=pltpu.CompilerParams(vmem_limit_bytes=32 << 20),
        cost_estimate=pl.CostEstimate(
            flops=400_000_000, bytes_accessed=4 << 20, transcendentals=0
        ),
    )(before, after, slope, edge, radius, radius, weight, total, out)


def weight_kernel(weight_ref, bias_ref, forward_ref, absolute_ref, backward_ref, ends_ref, tall_ref):
    c = weight_ref.shape[2]
    zero = jnp.zeros((c, c), F32)

    def place(ref, base, blocks):
        three = jnp.concatenate(blocks, axis=1)
        ref[pl.ds(base, c), :] = jnp.concatenate([three, zero], axis=1).astype(BF16)
        ref[pl.ds(base + c, c), :] = jnp.concatenate([zero, three], axis=1).astype(BF16)

    for j in range(3):
        turned = [weight_ref[i, j].T for i in range(3)]
        for ref, blocks in ((forward_ref, turned), (absolute_ref, [jnp.abs(w) for w in turned])):
            high = [w.astype(BF16).astype(F32) for w in blocks]
            place(ref, j * 2 * c, high)
            place(ref, (3 + j) * 2 * c, [w - h for w, h in zip(blocks, high)])
        place(backward_ref, j * 2 * c, [weight_ref[i, 2 - j] for i in (2, 1, 0)])
        for k, i in enumerate((2, 0)):
            ends_ref[k, pl.ds(j * c, c), :] = weight_ref[i, 2 - j].astype(BF16)
    tall = jnp.broadcast_to(bias_ref[...], (8, c)).T[:, :1]
    tall_ref[pl.ds(0, c), :] = tall
    tall_ref[pl.ds(c, c), :] = tall


def weight_pass(weight, bias):
    c = weight.shape[2]
    whole = lambda a: pl.BlockSpec(a.shape, lambda g, n=len(a.shape): (0,) * n)
    out = (
        jax.ShapeDtypeStruct((12 * c, 4 * c), BF16),
        jax.ShapeDtypeStruct((12 * c, 4 * c), BF16),
        jax.ShapeDtypeStruct((6 * c, 4 * c), BF16),
        jax.ShapeDtypeStruct((2, 3 * c, c), BF16),
        jax.ShapeDtypeStruct((2 * c, 1), F32),
    )
    bias = bias[None, :]
    return pl.pallas_call(
        weight_kernel,
        grid=(1,),
        out_shape=out,
        in_specs=[whole(weight), whole(bias)],
        out_specs=tuple(whole(a) for a in out),
    )(weight, bias)


def per_device(
    center, radius, conv_weight, conv_bias, split_status, out_coeffs, spec_ids, spec_offsets
):
    count, groups = (lax.axis_size("rows"), lax.axis_size("specs"))
    rows, columns, channels = center.shape
    center, radius, status = (jnp.swapaxes(a, 1, 2) for a in (center, radius, split_status))
    coeffs = jnp.swapaxes(out_coeffs, 2, 3)

    lanes = groups // SHARE
    me = lax.axis_index("specs")
    core, y = (lax.rem(me, 2), me // (2 * lanes))
    up = core == 0
    where = jnp.stack(
        [jnp.where(up, rows // 2 - 1, 0), y, jnp.where(up, rows - 1, 0)]
    ).astype(jnp.int32)
    box, last, first = send_pass(where, center, radius, status, coeffs)
    moves = []
    for r in range(count):
        for s in range(groups):
            other = r + (1 if s % 2 == 0 else -1)
            if 0 <= other < count:
                moves.append((r * groups + s, other * groups + s))
    box = lax.ppermute(box, ("rows", "specs"), moves)
    before = lax.ppermute(last, "rows", [(i, i + 1) for i in range(count - 1)])
    after = lax.ppermute(first, "rows", [(i + 1, i) for i in range(count - 1)])
    halo = lax.all_gather(
        box,
        "specs",
        axis_index_groups=[
            [(k * lanes + z) * 2 + e for k in range(SHARE // 2) for e in range(2)]
            for z in range(lanes)
        ],
    )

    forward, absolute, backward, ends, bias = weight_pass(conv_weight, conv_bias)
    out, edge, slope, total = main_pass(
        halo, center, radius, status, forward, absolute, backward, bias, coeffs
    )
    out, partial = edge_pass(before, after, slope, edge, radius, ends, total, out)

    step = 1
    while step < count:
        partial = partial + lax.ppermute(partial, "rows", [(i, i ^ step) for i in range(count)])
        step *= 2
    summed = jnp.sum(partial, axis=1)
    pixels = rows * count * columns
    entries = spec_offsets.shape[0]
    onehot = spec_ids[:, None] == jnp.arange(entries, dtype=jnp.int32)[None, :]
    table_terms = jnp.sum(jnp.where(onehot, spec_offsets[None, :], 0.0), axis=1)
    bounds = summed / pixels + table_terms
    return (jnp.swapaxes(out, 2, 3), bounds)


def solution(mesh):
    in_specs = (
        P("rows", None, None),
        P("rows", None, None),
        P(),
        P(),
        P("rows", None, None),
        P("specs", "rows", None, None),
        P("specs"),
        P(),
    )
    out_specs = (P("specs", "rows", None, None), P("specs"))
    return jax.shard_map(
        per_device, mesh=mesh, in_specs=in_specs, out_specs=out_specs, check_vma=False
    )
```

```python
import functools

import jax
import jax.numpy as jnp
from jax import lax
from jax.experimental import pallas as pl
from jax.experimental.pallas import tpu as pltpu
from jax.sharding import PartitionSpec as P

F32, BF16 = (jnp.float32, jnp.bfloat16)
SHARE = 8
MAIN_FLOPS = 0
EDGE_FLOPS = 5_000_000_000
MAIN_VMEM = 44 << 20
EDGE_VMEM = 8 << 20
UNITS = 7


def spread_columns(stack, columns):
    size = stack.shape[0] // 3
    where = lax.broadcasted_iota(jnp.int32, (size, columns), 1)
    right = pltpu.roll(stack[:size], 1, 1)
    left = pltpu.roll(stack[2 * size :], columns - 1, 1)
    right = jnp.where(where == 0, 0.0, right)
    left = jnp.where(where == columns - 1, 0.0, left)
    return right + stack[size : 2 * size] + left


def mul(a, b):
    return jnp.dot(a, b, preferred_element_type=F32)


def high_low(value):
    high = value.astype(BF16)
    return high, (value - high.astype(F32)).astype(BF16)


def edges_kernel(coeff_ref, last_ref, first_ref, held_ref, sems):
    specs, rows = coeff_ref.shape[:2]
    rows_of = ((rows - 1, last_ref), (0, first_ref))
    todo = [(k, s, h, ref) for k, (h, ref) in enumerate(rows_of) for s in range(specs)]
    reads = [
        pltpu.make_async_copy(coeff_ref.at[s, h], held_ref.at[k, s], sems.at[0, k, s])
        for k, s, h, _ in todo
    ]
    writes = [
        pltpu.make_async_copy(held_ref.at[k, s], ref.at[s], sems.at[1, k, s])
        for k, s, _, ref in todo
    ]
    for read in reads:
        read.start()
    for read, write in zip(reads, writes):
        read.wait()
        write.start()
    for write in writes:
        write.wait()


def edges_pass(coeffs):
    specs, rows, channels, columns = coeffs.shape
    edge = jax.ShapeDtypeStruct((specs, channels, columns), BF16)
    anywhere = pl.BlockSpec(memory_space=pl.ANY)
    return pl.pallas_call(
        edges_kernel,
        out_shape=(edge, edge),
        in_specs=[anywhere],
        out_specs=(anywhere, anywhere),
        scratch_shapes=[
            pltpu.VMEM((2, specs, channels, columns), BF16),
            pltpu.SemaphoreType.DMA((2, 2, specs)),
        ],
        cost_estimate=pl.CostEstimate(flops=0, bytes_accessed=4 << 20, transcendentals=0),
    )(coeffs)


def payload_kernel(where_ref, center_ref, radius_ref, status_ref, _, out_ref):
    high, low = high_low(center_ref[...])
    out_ref[0:2] = high
    out_ref[2:4] = low
    out_ref[4:6] = radius_ref[...].astype(BF16)
    out_ref[6:7] = status_ref[...].astype(F32).astype(BF16)


def payload_pass(where, center, radius, status, after):
    rows, channels, columns = center.shape
    part = channels * 2 // SHARE
    box = pl.BlockSpec((2, part, columns), lambda g, w: (w[0], w[1], 0))
    return pl.pallas_call(
        payload_kernel,
        out_shape=jax.ShapeDtypeStruct((UNITS, part, columns), BF16),
        grid_spec=pltpu.PrefetchScalarGridSpec(
            num_scalar_prefetch=1,
            grid=(1,),
            in_specs=[
                box,
                box,
                pl.BlockSpec((1, part, columns), lambda g, w: (w[2], w[1], 0)),
                pl.BlockSpec(memory_space=pl.ANY),
            ],
            out_specs=pl.BlockSpec((UNITS, part, columns), lambda g, w: (0, 0, 0)),
        ),
        cost_estimate=pl.CostEstimate(flops=0, bytes_accessed=1 << 20, transcendentals=0),
    )(where, center, radius, status, after)


def main_kernel(
    halo_ref,
    center_ref,
    radius_ref,
    status_ref,
    bands_ref,
    bias_ref,
    coeff_ref,
    out_ref,
    edge_ref,
    slope_edge_ref,
    total_ref,
    ch_ref,
    cl_ref,
    rh_ref,
    rl_ref,
    status_ext_ref,
    slope_ref,
    intercept_ref,
    linear_ref,
    pre_ref,
):
    rows, channels, columns = center_ref.shape
    c = channels
    part = halo_ref.shape[2]

    @pl.when(pl.program_id(0) == 0)
    def _():
        for side, base in ((0, 0), (1, rows + 2)):
            for y in range(c // part):
                piece = halo_ref.at[2 * y + side]
                for k in range(2):
                    at = pl.ds((base + k) * c + y * part, part)
                    ch_ref[at, :] = piece[k]
                    cl_ref[at, :] = piece[2 + k]
                    rh_ref[at, :] = piece[4 + k]
                    rl_ref[at, :] = jnp.zeros((part, columns), BF16)
                row = 0 if side == 0 else rows + 1
                status_ext_ref[pl.ds(row * c + y * part, part), :] = piece[6]
        for h in range(rows):
            at = pl.ds((h + 2) * c, c)
            ch_ref[at, :], cl_ref[at, :] = high_low(center_ref[h])
            rh_ref[at, :], rl_ref[at, :] = high_low(radius_ref[h])
            status_ext_ref[pl.ds((h + 1) * c, c), :] = status_ref[h].astype(F32).astype(BF16)
        pre_ref[pl.ds(0, c), :] = jnp.zeros((c, columns), BF16)
        pre_ref[pl.ds((rows + 1) * c, c), :] = jnp.zeros((c, columns), BF16)

        tall = jnp.broadcast_to(bias_ref[...], (8, c)).T[:, :1]
        tall = jnp.concatenate([tall, tall], axis=0)
        six = 6 * c

        @pl.loop(0, (rows + 2) // 2)
        def _(b):
            at = pl.ds(pl.multiple_of(b * 2 * c, 2 * c), 4 * c)
            here = pl.ds(pl.multiple_of(b * 2 * c, 2 * c), 2 * c)
            fh, fl, ah, al = (bands_ref[k * six : (k + 1) * six, :] for k in range(4))
            low = spread_columns(mul(fh, ch_ref[at, :]) + mul(fh, cl_ref[at, :]), columns)
            linear = low + tall
            center_out = linear + spread_columns(mul(fl, ch_ref[at, :]), columns)
            radius_out = spread_columns(
                mul(ah, rh_ref[at, :]) + mul(ah, rl_ref[at, :]) + mul(al, rh_ref[at, :]), columns
            )
            upper = center_out + radius_out
            lower = center_out - radius_out
            width = 2.0 * radius_out
            relaxed = jnp.minimum(jnp.maximum(upper, 0.0), width) / width
            status = status_ext_ref[here, :].astype(F32)
            open_ = status == 2.0
            slope = jnp.where(open_, relaxed, jnp.where(status == 1.0, 1.0, 0.0))
            slope_ref[here, :] = slope.astype(BF16)
            intercept = jnp.where(open_, -relaxed * jnp.minimum(lower, 0.0), 0.0)
            intercept_ref[here, :] = intercept.astype(BF16)
            linear_ref[here, :] = linear

        slope_edge_ref[0] = slope_ref[pl.ds(0, c), :]
        slope_edge_ref[1] = slope_ref[pl.ds((rows + 1) * c, c), :]

    total = jnp.zeros((8, columns), F32)
    for h in range(rows):
        at = pl.ds((h + 1) * c, c)
        coeff = coeff_ref[0, h]
        wide = coeff.astype(F32)
        pre = (wide * slope_ref[at, :].astype(F32)).astype(BF16)
        pre_ref[at, :] = pre
        terms = (
            jnp.minimum(wide, 0.0) * intercept_ref[at, :].astype(F32)
            + pre.astype(F32) * linear_ref[at, :]
        )
        total = total + jnp.sum(terms.reshape(c // 8, 8, columns), axis=0)

    for b in range(rows // 2):
        at = pl.ds(b * 2 * c, 4 * c)
        value = spread_columns(mul(bands_ref[24 * c :, :], pre_ref[at, :]), columns)
        for r in range(2):
            h = 2 * b + r
            row = value[r * c : (r + 1) * c]
            if h == 0 or h == rows - 1:
                edge_ref[0, 0 if h == 0 else 1] = row
            else:
                terms = jnp.abs(row) * radius_ref[h]
                total = total - jnp.sum(terms.reshape(c // 8, 8, columns), axis=0)
            out_ref[0, h] = row.astype(BF16)
    folded = total[:, :128]
    for k in range(1, columns // 128):
        folded = folded + total[:, k * 128 : (k + 1) * 128]
    total_ref[0] = folded


def main_pass(halo, center, radius, status, bands, bias, coeffs):
    specs, rows, channels, columns = coeffs.shape
    whole = lambda a: pl.BlockSpec(a.shape, lambda s, n=a.ndim: (0,) * n)
    ext = (rows + 4) * channels
    mid = (rows + 2) * channels
    return pl.pallas_call(
        main_kernel,
        grid=(specs,),
        out_shape=(
            jax.ShapeDtypeStruct(coeffs.shape, BF16),
            jax.ShapeDtypeStruct((specs, 2, channels, columns), F32),
            jax.ShapeDtypeStruct((2, channels, columns), BF16),
            jax.ShapeDtypeStruct((specs, 8, 128), F32),
        ),
        in_specs=[
            whole(a) for a in (halo, center, radius, status, bands, bias)
        ]
        + [pl.BlockSpec((1, rows, channels, columns), lambda s: (s, 0, 0, 0))],
        out_specs=(
            pl.BlockSpec((1, rows, channels, columns), lambda s: (s, 0, 0, 0)),
            pl.BlockSpec((1, 2, channels, columns), lambda s: (s, 0, 0, 0)),
            pl.BlockSpec((2, channels, columns), lambda s: (0, 0, 0)),
            pl.BlockSpec((1, 8, 128), lambda s: (s, 0, 0)),
        ),
        scratch_shapes=[pltpu.VMEM((ext, columns), BF16)] * 4
        + [
            pltpu.VMEM((mid, columns), BF16),
            pltpu.VMEM((mid, columns), BF16),
            pltpu.VMEM((mid, columns), BF16),
            pltpu.VMEM((mid, columns), F32),
            pltpu.VMEM((mid, columns), BF16),
        ],
        compiler_params=pltpu.CompilerParams(vmem_limit_bytes=MAIN_VMEM),
        cost_estimate=pl.CostEstimate(
            flops=MAIN_FLOPS, bytes_accessed=1024, transcendentals=0
        ),
    )(halo, center, radius, status, bands, bias, coeffs)


def edge_kernel(
    row,
    halo_ref,
    slope_ref,
    edge_ref,
    radius_ref,
    weight_ref,
    total_ref,
    _,
    out_ref,
    sum_ref,
    done_ref,
    sems,
):
    size, channels, columns = halo_ref.shape
    specs = out_ref.shape[0]
    step = pl.program_id(0)

    def store(s):
        return pltpu.make_async_copy(done_ref.at[s], out_ref.at[s, row], sems.at[s])

    for i in range(size):
        s = step * size + i
        pre = (halo_ref[i].astype(F32) * slope_ref[0].astype(F32)).astype(BF16)
        value = edge_ref[i, 0] + spread_columns(mul(weight_ref[0], pre), columns)
        done_ref[s] = value.astype(BF16)
        store(s).start()
        terms = jnp.abs(value) * radius_ref[0]
        terms = jnp.sum(terms.reshape(channels // 8, 8, columns), axis=0)
        folded = terms[:, :128]
        for m in range(1, columns // 128):
            folded = folded + terms[:, m * 128 : (m + 1) * 128]
        folded = total_ref[i] - folded
        if len(sum_ref.shape) == 3:
            sum_ref[i] = folded
        else:
            sum_ref[pl.ds(s, 1), :] = jnp.sum(folded, axis=0, keepdims=True)

    @pl.when(step == pl.num_programs(0) - 1)
    def _():
        for s in range(specs):
            store(s).wait()


def edge_pass(k, halo, slope, edge, radius, weight, total, out):
    specs, rows, channels, columns = out.shape
    size = 2
    row = 0 if k == 0 else rows - 1
    if k == 0:
        sums = jax.ShapeDtypeStruct(total.shape, F32)
        sums_spec = pl.BlockSpec((size, *total.shape[1:]), lambda g: (g, 0, 0))
    else:
        sums = jax.ShapeDtypeStruct((specs, 128), F32)
        sums_spec = pl.BlockSpec((specs, 128), lambda g: (0, 0))
    return pl.pallas_call(
        lambda *refs: edge_kernel(row, *refs),
        grid=(specs // size,),
        out_shape=(
            jax.ShapeDtypeStruct(out.shape, BF16),
            sums,
        ),
        in_specs=[
            pl.BlockSpec((size, channels, columns), lambda g: (g, 0, 0)),
            pl.BlockSpec((1, channels, columns), lambda g: (k, 0, 0)),
            pl.BlockSpec((size, 1, channels, columns), lambda g: (g, k, 0, 0)),
            pl.BlockSpec((1, channels, columns), lambda g: (row, 0, 0)),
            pl.BlockSpec((1, 3 * channels, channels), lambda g: (k, 0, 0)),
            pl.BlockSpec((size, *total.shape[1:]), lambda g: (g, 0, 0)),
            pl.BlockSpec(memory_space=pl.ANY),
        ],
        out_specs=(
            pl.BlockSpec(memory_space=pl.ANY),
            sums_spec,
        ),
        scratch_shapes=[
            pltpu.VMEM((specs, channels, columns), BF16),
            pltpu.SemaphoreType.DMA((specs,)),
        ],
        input_output_aliases={6: 0},
        compiler_params=pltpu.CompilerParams(vmem_limit_bytes=EDGE_VMEM),
        cost_estimate=pl.CostEstimate(
            flops=EDGE_FLOPS, bytes_accessed=1024, transcendentals=0
        ),
    )(halo, slope, edge, radius, weight, total, out)


def weight_kernel(weight_ref, bands_ref, ends_ref):
    c = weight_ref.shape[2]
    zero = jnp.zeros((c, c), F32)

    def place(base, blocks):
        three = jnp.concatenate(blocks, axis=1)
        bands_ref[pl.ds(base, c), :] = jnp.concatenate([three, zero], axis=1).astype(BF16)
        bands_ref[pl.ds(base + c, c), :] = jnp.concatenate([zero, three], axis=1).astype(BF16)

    for j in range(3):
        turned = [weight_ref[i, j].T for i in range(3)]
        for base, blocks in ((0, turned), (12 * c, [jnp.abs(w) for w in turned])):
            high = [w.astype(BF16).astype(F32) for w in blocks]
            place(base + j * 2 * c, high)
            place(base + (3 + j) * 2 * c, [w - h for w, h in zip(blocks, high)])
        place((12 + j) * 2 * c, [weight_ref[i, 2 - j] for i in (2, 1, 0)])
        for k, i in enumerate((2, 0)):
            ends_ref[k, pl.ds(j * c, c), :] = weight_ref[i, 2 - j].astype(BF16)


def weight_pass(weight):
    c = weight.shape[2]
    whole = lambda a: pl.BlockSpec(a.shape, lambda g, n=len(a.shape): (0,) * n)
    out = (
        jax.ShapeDtypeStruct((30 * c, 4 * c), BF16),
        jax.ShapeDtypeStruct((2, 3 * c, c), BF16),
    )
    return pl.pallas_call(
        weight_kernel,
        grid=(1,),
        out_shape=out,
        in_specs=[whole(weight)],
        out_specs=tuple(whole(a) for a in out),
    )(weight)


def per_device(
    center, radius, conv_weight, conv_bias, split_status, out_coeffs, spec_ids, spec_offsets
):
    count, groups = (lax.axis_size("rows"), lax.axis_size("specs"))
    rows, columns, channels = center.shape
    center, radius, status = (jnp.swapaxes(a, 1, 2) for a in (center, radius, split_status))
    coeffs = jnp.swapaxes(out_coeffs, 2, 3)

    lanes = groups // SHARE
    me = lax.axis_index("specs")
    core, y = (lax.rem(me, 2), me // (2 * lanes))
    up = core == 0
    where = jnp.stack(
        [jnp.where(up, rows // 2 - 1, 0), y, jnp.where(up, rows - 1, 0)]
    ).astype(jnp.int32)
    last, first = edges_pass(coeffs)
    before = lax.ppermute(last, "rows", [(i, i + 1) for i in range(count - 1)])
    box = payload_pass(where, center, radius, status, last)
    moves = []
    for r in range(count):
        for s in range(groups):
            other = r + (1 if s % 2 == 0 else -1)
            if 0 <= other < count:
                moves.append((r * groups + s, other * groups + s))
    box = lax.ppermute(box, ("rows", "specs"), moves)
    after = lax.ppermute(first, "rows", [(i + 1, i) for i in range(count - 1)])
    halo = lax.all_gather(
        box,
        "specs",
        axis_index_groups=[
            [(k * lanes + z) * 2 + e for k in range(SHARE // 2) for e in range(2)]
            for z in range(lanes)
        ],
    )

    bands, ends = weight_pass(conv_weight)
    out, edge, slope, total = main_pass(
        halo, center, radius, status, bands, conv_bias[None, :], coeffs
    )
    out, total = edge_pass(0, before, slope, edge, radius, ends, total, out)
    out, partial = edge_pass(1, after, slope, edge, radius, ends, total, out)

    others = [
        lax.ppermute(partial, "rows", [(i, i ^ step) for i in range(count)])
        for step in range(1, count)
    ]
    pairs = [partial, *others]
    while len(pairs) > 1:
        pairs = [a + b for a, b in zip(pairs[::2], pairs[1::2])]
    summed = jnp.sum(pairs[0], axis=1)
    pixels = rows * count * columns
    entries = spec_offsets.shape[0]
    onehot = spec_ids[:, None] == jnp.arange(entries, dtype=jnp.int32)[None, :]
    table_terms = jnp.sum(jnp.where(onehot, spec_offsets[None, :], 0.0), axis=1)
    bounds = summed / pixels + table_terms
    return (jnp.swapaxes(out, 2, 3), bounds)


def solution(mesh):
    in_specs = (
        P("rows", None, None),
        P("rows", None, None),
        P(),
        P(),
        P("rows", None, None),
        P("specs", "rows", None, None),
        P("specs"),
        P(),
    )
    out_specs = (P("specs", "rows", None, None), P("specs"))
    return jax.shard_map(
        per_device, mesh=mesh, in_specs=in_specs, out_specs=out_specs, check_vma=False
    )
```

```python
import functools

import functools

import jax
import jax.numpy as jnp
from jax import lax
from jax.experimental import pallas as pl
from jax.experimental.pallas import tpu as pltpu
from jax.sharding import PartitionSpec as P

F32, BF16 = (jnp.float32, jnp.bfloat16)
SHARE = 8
MAIN_FLOPS = 20_000_000_000
EDGE_FLOPS = 2_000_000_000
MAIN_VMEM = 44 << 20
EDGE_VMEM = 8 << 20
UNITS = 5


def spread_columns(stack, columns):
    size = stack.shape[0] // 3
    where = lax.broadcasted_iota(jnp.int32, (size, columns), 1)
    right = pltpu.roll(stack[:size], 1, 1)
    left = pltpu.roll(stack[2 * size :], columns - 1, 1)
    right = jnp.where(where == 0, 0.0, right)
    left = jnp.where(where == columns - 1, 0.0, left)
    return right + stack[size : 2 * size] + left


def mul(a, b):
    return jnp.dot(a, b, preferred_element_type=F32)


def high_low(value):
    high = value.astype(BF16)
    return high, (value - high.astype(F32)).astype(BF16)


def payload_kernel(where_ref, center_ref, radius_ref, status_ref, out_ref):
    out_ref[0:2] = center_ref[...].astype(BF16)
    out_ref[2:4] = radius_ref[...].astype(BF16)
    out_ref[4:5] = status_ref[...].astype(F32).astype(BF16)


def payload_pass(where, center, radius, status):
    rows, channels, columns = center.shape
    part = channels * 2 // SHARE
    box = pl.BlockSpec((2, part, columns), lambda g, w: (w[0], w[1], 0))
    return pl.pallas_call(
        payload_kernel,
        out_shape=jax.ShapeDtypeStruct((UNITS, part, columns), BF16),
        grid_spec=pltpu.PrefetchScalarGridSpec(
            num_scalar_prefetch=1,
            grid=(1,),
            in_specs=[
                box,
                box,
                pl.BlockSpec((1, part, columns), lambda g, w: (w[2], w[1], 0)),
            ],
            out_specs=pl.BlockSpec((UNITS, part, columns), lambda g, w: (0, 0, 0)),
        ),
        cost_estimate=pl.CostEstimate(flops=0, bytes_accessed=1 << 20, transcendentals=0),
    )(where, center, radius, status)


def send_kernel(sites_ref, coeff_ref, _, first_ref, second_ref, held_ref, sems):
    specs, rows = coeff_ref.shape[:2]
    todo = [
        (k, s, sites_ref[3 + k] * (rows - 1), ref)
        for k, ref in enumerate((first_ref, second_ref))
        for s in range(specs)
    ]
    reads = [
        pltpu.make_async_copy(coeff_ref.at[s, h], held_ref.at[k, s], sems.at[0, k, s])
        for k, s, h, _ in todo
    ]
    writes = [
        pltpu.make_async_copy(held_ref.at[k, s], ref.at[s], sems.at[1, k, s])
        for k, s, _, ref in todo
    ]
    for read in reads:
        read.start()
    for read, write in zip(reads, writes):
        read.wait()
        write.start()
    for write in writes:
        write.wait()


def send_pass(sites, coeffs, after):
    specs, rows, channels, columns = coeffs.shape
    edge = jax.ShapeDtypeStruct((specs, channels, columns), BF16)
    anywhere = pl.BlockSpec(memory_space=pl.ANY)
    return pl.pallas_call(
        send_kernel,
        out_shape=(edge, edge),
        grid_spec=pltpu.PrefetchScalarGridSpec(
            num_scalar_prefetch=1,
            grid=(1,),
            in_specs=[anywhere, anywhere],
            out_specs=(anywhere, anywhere),
            scratch_shapes=[
                pltpu.VMEM((2, specs, channels, columns), BF16),
                pltpu.SemaphoreType.DMA((2, 2, specs)),
            ],
        ),
        cost_estimate=pl.CostEstimate(flops=0, bytes_accessed=4 << 20, transcendentals=0),
    )(sites, coeffs, after)


def main_kernel(
    halo_ref,
    center_ref,
    radius_ref,
    status_ref,
    bands_ref,
    bias_ref,
    coeff_ref,
    out_ref,
    edge_ref,
    slope_edge_ref,
    total_ref,
    ch_ref,
    cl_ref,
    rh_ref,
    rl_ref,
    status_ext_ref,
    slope_ref,
    intercept_ref,
    linear_ref,
    pre_ref,
):
    rows, channels, columns = center_ref.shape
    c = channels
    part = halo_ref.shape[2]

    @pl.when(pl.program_id(0) == 0)
    def _():
        for side, base in ((0, 0), (1, rows + 2)):
            for y in range(c // part):
                piece = halo_ref.at[2 * y + side]
                for k in range(2):
                    at = pl.ds((base + k) * c + y * part, part)
                    ch_ref[at, :] = piece[k]
                    rh_ref[at, :] = piece[2 + k]
                    cl_ref[at, :] = jnp.zeros((part, columns), BF16)
                    rl_ref[at, :] = jnp.zeros((part, columns), BF16)
                row = 0 if side == 0 else rows + 1
                status_ext_ref[pl.ds(row * c + y * part, part), :] = piece[4]
        for h in range(rows):
            at = pl.ds((h + 2) * c, c)
            ch_ref[at, :], cl_ref[at, :] = high_low(center_ref[h])
            rh_ref[at, :], rl_ref[at, :] = high_low(radius_ref[h])
            status_ext_ref[pl.ds((h + 1) * c, c), :] = status_ref[h].astype(F32).astype(BF16)
        pre_ref[pl.ds(0, c), :] = jnp.zeros((c, columns), BF16)
        pre_ref[pl.ds((rows + 1) * c, c), :] = jnp.zeros((c, columns), BF16)

        tall = jnp.broadcast_to(bias_ref[...], (8, c)).T[:, :1]
        tall = jnp.concatenate([tall, tall], axis=0)
        six = 6 * c

        @pl.loop(0, (rows + 2) // 2)
        def _(b):
            at = pl.ds(pl.multiple_of(b * 2 * c, 2 * c), 4 * c)
            here = pl.ds(pl.multiple_of(b * 2 * c, 2 * c), 2 * c)
            fh, fl, ah, al = (bands_ref[k * six : (k + 1) * six, :] for k in range(4))
            low = spread_columns(mul(fh, ch_ref[at, :]) + mul(fh, cl_ref[at, :]), columns)
            linear = low + tall
            center_out = linear + spread_columns(mul(fl, ch_ref[at, :]), columns)
            radius_out = spread_columns(
                mul(ah, rh_ref[at, :]) + mul(ah, rl_ref[at, :]) + mul(al, rh_ref[at, :]), columns
            )
            upper = center_out + radius_out
            lower = center_out - radius_out
            width = 2.0 * radius_out
            relaxed = jnp.minimum(jnp.maximum(upper, 0.0), width) / width
            status = status_ext_ref[here, :].astype(F32)
            open_ = status == 2.0
            slope = jnp.where(open_, relaxed, jnp.where(status == 1.0, 1.0, 0.0))
            slope_ref[here, :] = slope.astype(BF16)
            intercept = jnp.where(open_, -relaxed * jnp.minimum(lower, 0.0), 0.0)
            intercept_ref[here, :] = intercept.astype(BF16)
            linear_ref[here, :] = linear

        slope_edge_ref[0] = slope_ref[pl.ds(0, c), :]
        slope_edge_ref[1] = slope_ref[pl.ds((rows + 1) * c, c), :]

    total = jnp.zeros((8, columns), F32)
    for h in range(rows):
        at = pl.ds((h + 1) * c, c)
        coeff = coeff_ref[0, h]
        wide = coeff.astype(F32)
        pre = (wide * slope_ref[at, :].astype(F32)).astype(BF16)
        pre_ref[at, :] = pre
        terms = (
            jnp.minimum(wide, 0.0) * intercept_ref[at, :].astype(F32)
            + pre.astype(F32) * linear_ref[at, :]
        )
        total = total + jnp.sum(terms.reshape(c // 8, 8, columns), axis=0)

    for b in range(rows // 2):
        at = pl.ds(b * 2 * c, 4 * c)
        value = spread_columns(mul(bands_ref[24 * c :, :], pre_ref[at, :]), columns)
        for r in range(2):
            h = 2 * b + r
            row = value[r * c : (r + 1) * c]
            if h == 0 or h == rows - 1:
                edge_ref[0, 0 if h == 0 else 1] = row
            else:
                terms = jnp.abs(row) * radius_ref[h]
                total = total - jnp.sum(terms.reshape(c // 8, 8, columns), axis=0)
            out_ref[0, h] = row.astype(BF16)
    folded = total[:, :128]
    for k in range(1, columns // 128):
        folded = folded + total[:, k * 128 : (k + 1) * 128]
    total_ref[0] = folded


def main_pass(halo, center, radius, status, bands, bias, coeffs):
    specs, rows, channels, columns = coeffs.shape
    whole = lambda a: pl.BlockSpec(a.shape, lambda s, n=a.ndim: (0,) * n)
    ext = (rows + 4) * channels
    mid = (rows + 2) * channels
    return pl.pallas_call(
        main_kernel,
        grid=(specs,),
        out_shape=(
            jax.ShapeDtypeStruct(coeffs.shape, BF16),
            jax.ShapeDtypeStruct((specs, 2, channels, columns), F32),
            jax.ShapeDtypeStruct((2, channels, columns), BF16),
            jax.ShapeDtypeStruct((specs, 8, 128), F32),
        ),
        in_specs=[
            whole(a) for a in (halo, center, radius, status, bands, bias)
        ]
        + [pl.BlockSpec((1, rows, channels, columns), lambda s: (s, 0, 0, 0))],
        out_specs=(
            pl.BlockSpec((1, rows, channels, columns), lambda s: (s, 0, 0, 0)),
            pl.BlockSpec((1, 2, channels, columns), lambda s: (s, 0, 0, 0)),
            pl.BlockSpec((2, channels, columns), lambda s: (0, 0, 0)),
            pl.BlockSpec((1, 8, 128), lambda s: (s, 0, 0)),
        ),
        scratch_shapes=[pltpu.VMEM((ext, columns), BF16)] * 4
        + [
            pltpu.VMEM((mid, columns), BF16),
            pltpu.VMEM((mid, columns), BF16),
            pltpu.VMEM((mid, columns), BF16),
            pltpu.VMEM((mid, columns), F32),
            pltpu.VMEM((mid, columns), BF16),
        ],
        compiler_params=pltpu.CompilerParams(vmem_limit_bytes=MAIN_VMEM),
        cost_estimate=pl.CostEstimate(
            flops=MAIN_FLOPS, bytes_accessed=16 << 20, transcendentals=0
        ),
    )(halo, center, radius, status, bands, bias, coeffs)


def edge_kernel(
    slot,
    sites_ref,
    halo_ref,
    slope_ref,
    edge_ref,
    radius_ref,
    weight_ref,
    total_ref,
    _,
    out_ref,
    sum_ref,
    done_ref,
    sems,
):
    specs, channels, columns = halo_ref.shape
    row = sites_ref[slot] * (out_ref.shape[1] - 1)

    def store(s):
        return pltpu.make_async_copy(done_ref.at[s], out_ref.at[s, row], sems.at[s])

    for s in range(specs):
        pre = (halo_ref[s].astype(F32) * slope_ref[0].astype(F32)).astype(BF16)
        value = edge_ref[s, 0] + spread_columns(mul(weight_ref[0], pre), columns)
        done_ref[s] = value.astype(BF16)
        store(s).start()
        terms = jnp.abs(value) * radius_ref[0]
        terms = jnp.sum(terms.reshape(channels // 8, 8, columns), axis=0)
        folded = terms[:, :128]
        for m in range(1, columns // 128):
            folded = folded + terms[:, m * 128 : (m + 1) * 128]
        folded = total_ref[s] - folded
        if len(sum_ref.shape) == 3:
            sum_ref[s] = folded
        else:
            sum_ref[s : s + 1, :] = jnp.sum(folded, axis=0, keepdims=True)
    for s in range(specs):
        store(s).wait()


def edge_pass(slot, sites, halo, slope, edge, radius, weight, total, out):
    specs, rows, channels, columns = out.shape
    last = slot == 4
    sums = (specs, 128) if last else total.shape
    return pl.pallas_call(
        functools.partial(edge_kernel, slot),
        out_shape=(
            jax.ShapeDtypeStruct(out.shape, BF16),
            jax.ShapeDtypeStruct(sums, F32),
        ),
        grid_spec=pltpu.PrefetchScalarGridSpec(
            num_scalar_prefetch=1,
            grid=(1,),
            in_specs=[
                pl.BlockSpec(halo.shape, lambda g, e: (0, 0, 0)),
                pl.BlockSpec((1, channels, columns), lambda g, e: (e[slot], 0, 0)),
                pl.BlockSpec((specs, 1, channels, columns), lambda g, e: (0, e[slot], 0, 0)),
                pl.BlockSpec((1, channels, columns), lambda g, e: (e[slot] * (rows - 1), 0, 0)),
                pl.BlockSpec((1, 3 * channels, channels), lambda g, e: (e[slot], 0, 0)),
                pl.BlockSpec(total.shape, lambda g, e: (0, 0, 0)),
                pl.BlockSpec(memory_space=pl.ANY),
            ],
            out_specs=(
                pl.BlockSpec(memory_space=pl.ANY),
                pl.BlockSpec(sums, lambda g, e: (0,) * len(sums)),
            ),
            scratch_shapes=[
                pltpu.VMEM((specs, channels, columns), BF16),
                pltpu.SemaphoreType.DMA((specs,)),
            ],
        ),
        input_output_aliases={7: 0},
        compiler_params=pltpu.CompilerParams(vmem_limit_bytes=EDGE_VMEM),
        cost_estimate=pl.CostEstimate(
            flops=EDGE_FLOPS, bytes_accessed=1 << 20, transcendentals=0
        ),
    )(sites, halo, slope, edge, radius, weight, total, out)


def weight_kernel(weight_ref, bands_ref, ends_ref):
    c = weight_ref.shape[2]
    zero = jnp.zeros((c, c), F32)

    def place(base, blocks):
        three = jnp.concatenate(blocks, axis=1)
        bands_ref[pl.ds(base, c), :] = jnp.concatenate([three, zero], axis=1).astype(BF16)
        bands_ref[pl.ds(base + c, c), :] = jnp.concatenate([zero, three], axis=1).astype(BF16)

    for j in range(3):
        turned = [weight_ref[i, j].T for i in range(3)]
        for base, blocks in ((0, turned), (12 * c, [jnp.abs(w) for w in turned])):
            high = [w.astype(BF16).astype(F32) for w in blocks]
            place(base + j * 2 * c, high)
            place(base + (3 + j) * 2 * c, [w - h for w, h in zip(blocks, high)])
        place((12 + j) * 2 * c, [weight_ref[i, 2 - j] for i in (2, 1, 0)])
        for k, i in enumerate((2, 0)):
            ends_ref[k, pl.ds(j * c, c), :] = weight_ref[i, 2 - j].astype(BF16)


def weight_pass(weight):
    c = weight.shape[2]
    whole = lambda a: pl.BlockSpec(a.shape, lambda g, n=len(a.shape): (0,) * n)
    out = (
        jax.ShapeDtypeStruct((30 * c, 4 * c), BF16),
        jax.ShapeDtypeStruct((2, 3 * c, c), BF16),
    )
    return pl.pallas_call(
        weight_kernel,
        grid=(1,),
        out_shape=out,
        in_specs=[whole(weight)],
        out_specs=tuple(whole(a) for a in out),
    )(weight)


def per_device(
    center, radius, conv_weight, conv_bias, split_status, out_coeffs, spec_ids, spec_offsets
):
    count, groups = (lax.axis_size("rows"), lax.axis_size("specs"))
    rows, columns, channels = center.shape
    center, radius, status = (jnp.swapaxes(a, 1, 2) for a in (center, radius, split_status))
    coeffs = jnp.swapaxes(out_coeffs, 2, 3)

    lanes = groups // SHARE
    me = lax.axis_index("specs")
    core, y = (lax.rem(me, 2), me // (2 * lanes))
    up = core == 0
    even = 1 - lax.rem(lax.axis_index("rows"), 2)
    sites = jnp.stack(
        [jnp.where(up, rows // 2 - 1, 0), y, jnp.where(up, rows - 1, 0), even, 1 - even]
    ).astype(jnp.int32)
    mine = payload_pass(sites, center, radius, status)
    moves = []
    for r in range(count):
        for s in range(groups):
            other = r + (1 if s % 2 == 0 else -1)
            if 0 <= other < count:
                moves.append((r * groups + s, other * groups + s))
    box = lax.ppermute(mine, ("rows", "specs"), moves)
    one, two = send_pass(sites, coeffs, mine)
    pairs = [(i, i + 1) for i in range(count - 1)]
    one = lax.ppermute(one, "rows", [m for p in pairs[::2] for m in (p, p[::-1])])
    two = lax.ppermute(two, "rows", [m for p in pairs[1::2] for m in (p, p[::-1])])
    halo = lax.all_gather(
        box,
        "specs",
        axis_index_groups=[
            [(k * lanes + z) * 2 + e for k in range(SHARE // 2) for e in range(2)]
            for z in range(lanes)
        ],
    )

    bands, ends = weight_pass(conv_weight)
    out, edge, slope, total = main_pass(
        halo, center, radius, status, bands, conv_bias[None, :], coeffs
    )
    out, total = edge_pass(3, sites, one, slope, edge, radius, ends, total, out)
    out, partial = edge_pass(4, sites, two, slope, edge, radius, ends, total, out)

    step = 1
    while step < count:
        partial = partial + lax.ppermute(partial, "rows", [(i, i ^ step) for i in range(count)])
        step *= 2
    summed = jnp.sum(partial, axis=1)
    pixels = rows * count * columns
    entries = spec_offsets.shape[0]
    onehot = spec_ids[:, None] == jnp.arange(entries, dtype=jnp.int32)[None, :]
    table_terms = jnp.sum(jnp.where(onehot, spec_offsets[None, :], 0.0), axis=1)
    bounds = summed / pixels + table_terms
    return (jnp.swapaxes(out, 2, 3), bounds)


def solution(mesh):
    in_specs = (
        P("rows", None, None),
        P("rows", None, None),
        P(),
        P(),
        P("rows", None, None),
        P("specs", "rows", None, None),
        P("specs"),
        P(),
    )
    out_specs = (P("specs", "rows", None, None), P("specs"))
    return jax.shard_map(
        per_device, mesh=mesh, in_specs=in_specs, out_specs=out_specs, check_vma=False
    )
```

```python
import functools

import functools

import jax
import jax.numpy as jnp
from jax import lax
from jax.experimental import pallas as pl
from jax.experimental.pallas import tpu as pltpu
from jax.sharding import PartitionSpec as P

F32, BF16 = (jnp.float32, jnp.bfloat16)
SHARE = 8
MAIN_FLOPS = 20_000_000_000
EDGE_FLOPS = 2_000_000_000
MAIN_VMEM = 44 << 20
EDGE_VMEM = 14 << 20
UNITS = 5


def spread_columns(stack, columns):
    size = stack.shape[0] // 3
    where = lax.broadcasted_iota(jnp.int32, (size, columns), 1)
    right = pltpu.roll(stack[:size], 1, 1)
    left = pltpu.roll(stack[2 * size :], columns - 1, 1)
    right = jnp.where(where == 0, 0.0, right)
    left = jnp.where(where == columns - 1, 0.0, left)
    return right + stack[size : 2 * size] + left


def mul(a, b):
    return jnp.dot(a, b, preferred_element_type=F32)


def high_low(value):
    high = value.astype(BF16)
    return high, (value - high.astype(F32)).astype(BF16)


def payload_kernel(
    lanes, center_ref, radius_ref, status_ref, box_ref, center_box, radius_box, status_box, sems
):
    rows = center_ref.shape[0]
    part = box_ref.shape[1]
    me = lax.axis_index("specs")
    up = 1 - lax.rem(me, 2)
    here = pl.ds(pl.multiple_of(me // (2 * lanes) * part, part), part)
    two = pl.ds(up * (rows - 2), 2)
    one = pl.ds(up * (rows - 1), 1)
    copies = [
        pltpu.make_async_copy(center_ref.at[two, here], center_box, sems.at[0]),
        pltpu.make_async_copy(radius_ref.at[two, here], radius_box, sems.at[1]),
        pltpu.make_async_copy(status_ref.at[one, here], status_box, sems.at[2]),
    ]
    for copy in copies:
        copy.start()
    for copy in copies:
        copy.wait()
    box_ref[0:2] = center_box[...].astype(BF16)
    box_ref[2:4] = radius_box[...].astype(BF16)
    box_ref[4:5] = status_box[...].astype(F32).astype(BF16)


def payload_pass(lanes, center, radius, status):
    rows, channels, columns = center.shape
    part = channels * 2 // SHARE
    return pl.pallas_call(
        functools.partial(payload_kernel, lanes),
        out_shape=jax.ShapeDtypeStruct((UNITS, part, columns), BF16),
        in_specs=[pl.BlockSpec(memory_space=pl.ANY)] * 3,
        out_specs=pl.BlockSpec(memory_space=pltpu.VMEM),
        scratch_shapes=[
            pltpu.VMEM((2, part, columns), F32),
            pltpu.VMEM((2, part, columns), F32),
            pltpu.VMEM((1, part, columns), jnp.int32),
            pltpu.SemaphoreType.DMA((3,)),
        ],
        cost_estimate=pl.CostEstimate(flops=0, bytes_accessed=1 << 20, transcendentals=0),
    )(center, radius, status)


def send_kernel(coeff_ref, _, first_ref, second_ref, held_ref, sems):
    specs, rows = coeff_ref.shape[:2]
    odd = lax.rem(lax.axis_index("rows"), 2)
    todo = [
        (k, s, h * (rows - 1), ref)
        for k, (h, ref) in enumerate(((1 - odd, first_ref), (odd, second_ref)))
        for s in range(specs)
    ]
    reads = [
        pltpu.make_async_copy(coeff_ref.at[s, h], held_ref.at[k, s], sems.at[0, k, s])
        for k, s, h, _ in todo
    ]
    writes = [
        pltpu.make_async_copy(held_ref.at[k, s], ref.at[s], sems.at[1, k, s])
        for k, s, _, ref in todo
    ]
    for read in reads:
        read.start()
    for read, write in zip(reads, writes):
        read.wait()
        write.start()
    for write in writes:
        write.wait()


def send_pass(coeffs, after):
    specs, rows, channels, columns = coeffs.shape
    edge = jax.ShapeDtypeStruct((specs, channels, columns), BF16)
    anywhere = pl.BlockSpec(memory_space=pl.ANY)
    return pl.pallas_call(
        send_kernel,
        out_shape=(edge, edge),
        in_specs=[anywhere, anywhere],
        out_specs=(anywhere, anywhere),
        scratch_shapes=[
            pltpu.VMEM((2, specs, channels, columns), BF16),
            pltpu.SemaphoreType.DMA((2, 2, specs)),
        ],
        cost_estimate=pl.CostEstimate(flops=0, bytes_accessed=4 << 20, transcendentals=0),
    )(coeffs, after)


def main_kernel(
    halo_ref,
    center_ref,
    radius_ref,
    status_ref,
    bands_ref,
    bias_ref,
    coeff_ref,
    out_ref,
    edge_ref,
    slope_edge_ref,
    total_ref,
    ch_ref,
    cl_ref,
    rh_ref,
    rl_ref,
    status_ext_ref,
    slope_ref,
    intercept_ref,
    linear_ref,
    pre_ref,
):
    rows, channels, columns = center_ref.shape
    c = channels
    part = halo_ref.shape[2]

    @pl.when(pl.program_id(0) == 0)
    def _():
        for side, base in ((0, 0), (1, rows + 2)):
            for y in range(c // part):
                piece = halo_ref.at[2 * y + side]
                for k in range(2):
                    at = pl.ds((base + k) * c + y * part, part)
                    ch_ref[at, :] = piece[k]
                    rh_ref[at, :] = piece[2 + k]
                    cl_ref[at, :] = jnp.zeros((part, columns), BF16)
                    rl_ref[at, :] = jnp.zeros((part, columns), BF16)
                row = 0 if side == 0 else rows + 1
                status_ext_ref[pl.ds(row * c + y * part, part), :] = piece[4]
        for h in range(rows):
            at = pl.ds((h + 2) * c, c)
            ch_ref[at, :], cl_ref[at, :] = high_low(center_ref[h])
            rh_ref[at, :], rl_ref[at, :] = high_low(radius_ref[h])
            status_ext_ref[pl.ds((h + 1) * c, c), :] = status_ref[h].astype(F32).astype(BF16)
        pre_ref[pl.ds(0, c), :] = jnp.zeros((c, columns), BF16)
        pre_ref[pl.ds((rows + 1) * c, c), :] = jnp.zeros((c, columns), BF16)

        tall = jnp.broadcast_to(bias_ref[...], (8, c)).T[:, :1]
        tall = jnp.concatenate([tall, tall], axis=0)
        six = 6 * c

        @pl.loop(0, (rows + 2) // 2)
        def _(b):
            at = pl.ds(pl.multiple_of(b * 2 * c, 2 * c), 4 * c)
            here = pl.ds(pl.multiple_of(b * 2 * c, 2 * c), 2 * c)
            fh, fl, ah, al = (bands_ref[k * six : (k + 1) * six, :] for k in range(4))
            low = spread_columns(mul(fh, ch_ref[at, :]) + mul(fh, cl_ref[at, :]), columns)
            linear = low + tall
            center_out = linear + spread_columns(mul(fl, ch_ref[at, :]), columns)
            radius_out = spread_columns(
                mul(ah, rh_ref[at, :]) + mul(ah, rl_ref[at, :]) + mul(al, rh_ref[at, :]), columns
            )
            upper = center_out + radius_out
            lower = center_out - radius_out
            width = 2.0 * radius_out
            relaxed = jnp.minimum(jnp.maximum(upper, 0.0), width) / width
            status = status_ext_ref[here, :].astype(F32)
            open_ = status == 2.0
            slope = jnp.where(open_, relaxed, jnp.where(status == 1.0, 1.0, 0.0))
            slope_ref[here, :] = slope.astype(BF16)
            intercept = jnp.where(open_, -relaxed * jnp.minimum(lower, 0.0), 0.0)
            intercept_ref[here, :] = intercept.astype(BF16)
            linear_ref[here, :] = linear

        slope_edge_ref[0] = slope_ref[pl.ds(0, c), :]
        slope_edge_ref[1] = slope_ref[pl.ds((rows + 1) * c, c), :]

    total = jnp.zeros((8, columns), F32)
    for h in range(rows):
        at = pl.ds((h + 1) * c, c)
        coeff = coeff_ref[0, h]
        wide = coeff.astype(F32)
        pre = (wide * slope_ref[at, :].astype(F32)).astype(BF16)
        pre_ref[at, :] = pre
        terms = (
            jnp.minimum(wide, 0.0) * intercept_ref[at, :].astype(F32)
            + pre.astype(F32) * linear_ref[at, :]
        )
        total = total + jnp.sum(terms.reshape(c // 8, 8, columns), axis=0)

    for b in range(rows // 2):
        at = pl.ds(b * 2 * c, 4 * c)
        value = spread_columns(mul(bands_ref[24 * c :, :], pre_ref[at, :]), columns)
        for r in range(2):
            h = 2 * b + r
            row = value[r * c : (r + 1) * c]
            if h == 0 or h == rows - 1:
                edge_ref[0, 0 if h == 0 else 1] = row
            else:
                terms = jnp.abs(row) * radius_ref[h]
                total = total - jnp.sum(terms.reshape(c // 8, 8, columns), axis=0)
            out_ref[0, h] = row.astype(BF16)
    folded = total[:, :128]
    for k in range(1, columns // 128):
        folded = folded + total[:, k * 128 : (k + 1) * 128]
    total_ref[0] = folded


def main_pass(halo, center, radius, status, bands, bias, coeffs):
    specs, rows, channels, columns = coeffs.shape
    whole = lambda a: pl.BlockSpec(a.shape, lambda s, n=a.ndim: (0,) * n)
    ext = (rows + 4) * channels
    mid = (rows + 2) * channels
    return pl.pallas_call(
        main_kernel,
        grid=(specs,),
        out_shape=(
            jax.ShapeDtypeStruct(coeffs.shape, BF16),
            jax.ShapeDtypeStruct((specs, 2, channels, columns), F32),
            jax.ShapeDtypeStruct((2, channels, columns), BF16),
            jax.ShapeDtypeStruct((specs, 8, 128), F32),
        ),
        in_specs=[
            whole(a) for a in (halo, center, radius, status, bands, bias)
        ]
        + [pl.BlockSpec((1, rows, channels, columns), lambda s: (s, 0, 0, 0))],
        out_specs=(
            pl.BlockSpec((1, rows, channels, columns), lambda s: (s, 0, 0, 0)),
            pl.BlockSpec((1, 2, channels, columns), lambda s: (s, 0, 0, 0)),
            pl.BlockSpec((2, channels, columns), lambda s: (0, 0, 0)),
            pl.BlockSpec((1, 8, 128), lambda s: (s, 0, 0)),
        ),
        scratch_shapes=[pltpu.VMEM((ext, columns), BF16)] * 4
        + [
            pltpu.VMEM((mid, columns), BF16),
            pltpu.VMEM((mid, columns), BF16),
            pltpu.VMEM((mid, columns), BF16),
            pltpu.VMEM((mid, columns), F32),
            pltpu.VMEM((mid, columns), BF16),
        ],
        compiler_params=pltpu.CompilerParams(vmem_limit_bytes=MAIN_VMEM),
        cost_estimate=pl.CostEstimate(
            flops=MAIN_FLOPS, bytes_accessed=16 << 20, transcendentals=0
        ),
    )(halo, center, radius, status, bands, bias, coeffs)


def edge_kernel(
    sites_ref,
    one_ref,
    two_ref,
    slope_ref,
    edge_ref,
    radius_one_ref,
    radius_two_ref,
    weight_ref,
    total_ref,
    _,
    out_ref,
    sum_ref,
    done_ref,
    sems,
):
    specs, channels, columns = one_ref.shape
    rows = out_ref.shape[1]

    def store(s, k):
        row = sites_ref[k] * (rows - 1)
        return pltpu.make_async_copy(done_ref.at[s, k], out_ref.at[s, row], sems.at[s, k])

    for s in range(specs):
        total = total_ref[s]
        for k, (halo_ref, radius_ref) in enumerate(
            ((one_ref, radius_one_ref), (two_ref, radius_two_ref))
        ):
            e = sites_ref[k]
            pre = (halo_ref[s].astype(F32) * slope_ref[e].astype(F32)).astype(BF16)
            value = edge_ref[s, e] + spread_columns(mul(weight_ref[e], pre), columns)
            done_ref[s, k] = value.astype(BF16)
            store(s, k).start()
            terms = jnp.abs(value) * radius_ref[0]
            terms = jnp.sum(terms.reshape(channels // 8, 8, columns), axis=0)
            for m in range(columns // 128):
                total = total - terms[:, m * 128 : (m + 1) * 128]
        sum_ref[s : s + 1, :] = jnp.sum(total, axis=0, keepdims=True)
    for s in range(specs):
        for k in range(2):
            store(s, k).wait()


def edge_pass(sites, one, two, slope, edge, radius, weight, total, out):
    specs, rows, channels, columns = out.shape
    whole = lambda a: pl.BlockSpec(a.shape, lambda g, e, n=a.ndim: (0,) * n)
    return pl.pallas_call(
        edge_kernel,
        out_shape=(
            jax.ShapeDtypeStruct(out.shape, BF16),
            jax.ShapeDtypeStruct((specs, 128), F32),
        ),
        grid_spec=pltpu.PrefetchScalarGridSpec(
            num_scalar_prefetch=1,
            grid=(1,),
            in_specs=[
                whole(one),
                whole(two),
                whole(slope),
                whole(edge),
                pl.BlockSpec((1, channels, columns), lambda g, e: (e[0] * (rows - 1), 0, 0)),
                pl.BlockSpec((1, channels, columns), lambda g, e: (e[1] * (rows - 1), 0, 0)),
                whole(weight),
                whole(total),
                pl.BlockSpec(memory_space=pl.ANY),
            ],
            out_specs=(
                pl.BlockSpec(memory_space=pl.ANY),
                pl.BlockSpec((specs, 128), lambda g, e: (0, 0)),
            ),
            scratch_shapes=[
                pltpu.VMEM((specs, 2, channels, columns), BF16),
                pltpu.SemaphoreType.DMA((specs, 2)),
            ],
        ),
        input_output_aliases={9: 0},
        compiler_params=pltpu.CompilerParams(vmem_limit_bytes=EDGE_VMEM),
        cost_estimate=pl.CostEstimate(
            flops=EDGE_FLOPS, bytes_accessed=1 << 20, transcendentals=0
        ),
    )(sites, one, two, slope, edge, radius, radius, weight, total, out)


def weight_kernel(weight_ref, bands_ref, ends_ref):
    c = weight_ref.shape[2]
    zero = jnp.zeros((c, c), F32)

    def place(base, blocks):
        three = jnp.concatenate(blocks, axis=1)
        bands_ref[pl.ds(base, c), :] = jnp.concatenate([three, zero], axis=1).astype(BF16)
        bands_ref[pl.ds(base + c, c), :] = jnp.concatenate([zero, three], axis=1).astype(BF16)

    for j in range(3):
        turned = [weight_ref[i, j].T for i in range(3)]
        for base, blocks in ((0, turned), (12 * c, [jnp.abs(w) for w in turned])):
            high = [w.astype(BF16).astype(F32) for w in blocks]
            place(base + j * 2 * c, high)
            place(base + (3 + j) * 2 * c, [w - h for w, h in zip(blocks, high)])
        place((12 + j) * 2 * c, [weight_ref[i, 2 - j] for i in (2, 1, 0)])
        for k, i in enumerate((2, 0)):
            ends_ref[k, pl.ds(j * c, c), :] = weight_ref[i, 2 - j].astype(BF16)


def weight_pass(weight):
    c = weight.shape[2]
    whole = lambda a: pl.BlockSpec(a.shape, lambda g, n=len(a.shape): (0,) * n)
    out = (
        jax.ShapeDtypeStruct((30 * c, 4 * c), BF16),
        jax.ShapeDtypeStruct((2, 3 * c, c), BF16),
    )
    return pl.pallas_call(
        weight_kernel,
        grid=(1,),
        out_shape=out,
        in_specs=[whole(weight)],
        out_specs=tuple(whole(a) for a in out),
    )(weight)


def per_device(
    center, radius, conv_weight, conv_bias, split_status, out_coeffs, spec_ids, spec_offsets
):
    count, groups = (lax.axis_size("rows"), lax.axis_size("specs"))
    rows, columns, channels = center.shape
    center, radius, status = (jnp.swapaxes(a, 1, 2) for a in (center, radius, split_status))
    coeffs = jnp.swapaxes(out_coeffs, 2, 3)

    lanes = groups // SHARE
    mine = payload_pass(lanes, center, radius, status)
    center, radius, status, mine = lax.optimization_barrier((center, radius, status, mine))
    moves = []
    for r in range(count):
        for s in range(groups):
            other = r + (1 if s % 2 == 0 else -1)
            if 0 <= other < count:
                moves.append((r * groups + s, other * groups + s))
    box = lax.ppermute(mine, ("rows", "specs"), moves)
    one, two = send_pass(coeffs, mine)
    pairs = [(i, i + 1) for i in range(count - 1)]
    one = lax.ppermute(one, "rows", [m for p in pairs[::2] for m in (p, p[::-1])])
    two = lax.ppermute(two, "rows", [m for p in pairs[1::2] for m in (p, p[::-1])])
    halo = lax.all_gather(
        box,
        "specs",
        axis_index_groups=[
            [(k * lanes + z) * 2 + e for k in range(SHARE // 2) for e in range(2)]
            for z in range(lanes)
        ],
    )

    bands, ends = weight_pass(conv_weight)
    out, edge, slope, total = main_pass(
        halo, center, radius, status, bands, conv_bias[None, :], coeffs
    )
    odd = lax.rem(lax.axis_index("rows"), 2)
    sites = jnp.stack([1 - odd, odd]).astype(jnp.int32)
    out, partial = edge_pass(sites, one, two, slope, edge, radius, ends, total, out)

    partial = partial + lax.ppermute(partial, "rows", [(i, i ^ 1) for i in range(count)])
    pairs = [partial] + [
        lax.ppermute(partial, "rows", [(i, i ^ step) for i in range(count)])
        for step in range(2, count, 2)
    ]
    while len(pairs) > 1:
        pairs = [a + b for a, b in zip(pairs[::2], pairs[1::2])]
    summed = jnp.sum(pairs[0], axis=1)
    pixels = rows * count * columns
    entries = spec_offsets.shape[0]
    onehot = spec_ids[:, None] == jnp.arange(entries, dtype=jnp.int32)[None, :]
    table_terms = jnp.sum(jnp.where(onehot, spec_offsets[None, :], 0.0), axis=1)
    bounds = summed / pixels + table_terms
    return (jnp.swapaxes(out, 2, 3), bounds)


def solution(mesh):
    in_specs = (
        P("rows", None, None),
        P("rows", None, None),
        P(),
        P(),
        P("rows", None, None),
        P("specs", "rows", None, None),
        P("specs"),
        P(),
    )
    out_specs = (P("specs", "rows", None, None), P("specs"))
    return jax.shard_map(
        per_device, mesh=mesh, in_specs=in_specs, out_specs=out_specs, check_vma=False
    )
```

```python
import functools

import functools

import jax
import jax.numpy as jnp
from jax import lax
from jax.experimental import pallas as pl
from jax.experimental.pallas import tpu as pltpu
from jax.sharding import PartitionSpec as P

F32, BF16 = (jnp.float32, jnp.bfloat16)
SHARE = 8
MAIN_FLOPS = 20_000_000_000
EDGE_FLOPS = 2_000_000_000
MAIN_VMEM = 44 << 20
EDGE_VMEM = 14 << 20
UNITS = 5


def spread_columns(stack, columns):
    size = stack.shape[0] // 3
    where = lax.broadcasted_iota(jnp.int32, (size, columns), 1)
    right = pltpu.roll(stack[:size], 1, 1)
    left = pltpu.roll(stack[2 * size :], columns - 1, 1)
    right = jnp.where(where == 0, 0.0, right)
    left = jnp.where(where == columns - 1, 0.0, left)
    return right + stack[size : 2 * size] + left


def mul(a, b):
    return jnp.dot(a, b, preferred_element_type=F32)


def high_low(value):
    high = value.astype(BF16)
    return high, (value - high.astype(F32)).astype(BF16)


def send_kernel(
    lanes,
    center_ref,
    radius_ref,
    status_ref,
    coeff_ref,
    box_ref,
    first_ref,
    second_ref,
    held_ref,
    center_box,
    radius_box,
    status_box,
    box_sems,
    sems,
):
    specs, rows = coeff_ref.shape[:2]
    part = box_ref.shape[1]
    me = lax.axis_index("specs")
    up = 1 - lax.rem(me, 2)
    here = pl.ds(pl.multiple_of(me // (2 * lanes) * part, part), part)
    two = pl.ds(up * (rows - 2), 2)
    one = pl.ds(up * (rows - 1), 1)
    odd = lax.rem(lax.axis_index("rows"), 2)
    boxes = [
        pltpu.make_async_copy(center_ref.at[two, here], center_box, box_sems.at[0]),
        pltpu.make_async_copy(radius_ref.at[two, here], radius_box, box_sems.at[1]),
        pltpu.make_async_copy(status_ref.at[one, here], status_box, box_sems.at[2]),
    ]
    todo = [
        (k, s, h * (rows - 1), ref)
        for k, (h, ref) in enumerate(((1 - odd, first_ref), (odd, second_ref)))
        for s in range(specs)
    ]
    reads = [
        pltpu.make_async_copy(coeff_ref.at[s, h], held_ref.at[k, s], sems.at[0, k, s])
        for k, s, h, _ in todo
    ]
    writes = [
        pltpu.make_async_copy(held_ref.at[k, s], ref.at[s], sems.at[1, k, s])
        for k, s, _, ref in todo
    ]
    for copy in boxes + reads:
        copy.start()
    for copy in boxes:
        copy.wait()
    box_ref[0:2] = center_box[...].astype(BF16)
    box_ref[2:4] = radius_box[...].astype(BF16)
    box_ref[4:5] = status_box[...].astype(F32).astype(BF16)
    for read, write in zip(reads, writes):
        read.wait()
        write.start()
    for write in writes:
        write.wait()


def send_pass(lanes, center, radius, status, coeffs):
    specs, rows, channels, columns = coeffs.shape
    part = channels * 2 // SHARE
    edge = jax.ShapeDtypeStruct((specs, channels, columns), BF16)
    anywhere = pl.BlockSpec(memory_space=pl.ANY)
    return pl.pallas_call(
        functools.partial(send_kernel, lanes),
        out_shape=(jax.ShapeDtypeStruct((UNITS, part, columns), BF16), edge, edge),
        in_specs=[anywhere] * 4,
        out_specs=(pl.BlockSpec(memory_space=pltpu.VMEM), anywhere, anywhere),
        scratch_shapes=[
            pltpu.VMEM((2, specs, channels, columns), BF16),
            pltpu.VMEM((2, part, columns), F32),
            pltpu.VMEM((2, part, columns), F32),
            pltpu.VMEM((1, part, columns), jnp.int32),
            pltpu.SemaphoreType.DMA((3,)),
            pltpu.SemaphoreType.DMA((2, 2, specs)),
        ],
        cost_estimate=pl.CostEstimate(flops=0, bytes_accessed=4 << 20, transcendentals=0),
    )(center, radius, status, coeffs)


def later_pass(first, second, box):
    def kernel(*refs):
        pass

    anywhere = pl.BlockSpec(memory_space=pl.ANY)
    return pl.pallas_call(
        kernel,
        out_shape=tuple(jax.ShapeDtypeStruct(a.shape, a.dtype) for a in (first, second)),
        in_specs=[anywhere] * 3,
        out_specs=(anywhere, anywhere),
        input_output_aliases={0: 0, 1: 1},
    )(first, second, box)


def main_kernel(
    halo_ref,
    center_ref,
    radius_ref,
    status_ref,
    bands_ref,
    bias_ref,
    coeff_ref,
    out_ref,
    edge_ref,
    slope_edge_ref,
    total_ref,
    ch_ref,
    cl_ref,
    rh_ref,
    rl_ref,
    status_ext_ref,
    slope_ref,
    intercept_ref,
    linear_ref,
    pre_ref,
):
    rows, channels, columns = center_ref.shape
    c = channels
    part = halo_ref.shape[2]

    @pl.when(pl.program_id(0) == 0)
    def _():
        for side, base in ((0, 0), (1, rows + 2)):
            for y in range(c // part):
                piece = halo_ref.at[2 * y + side]
                for k in range(2):
                    at = pl.ds((base + k) * c + y * part, part)
                    ch_ref[at, :] = piece[k]
                    rh_ref[at, :] = piece[2 + k]
                    cl_ref[at, :] = jnp.zeros((part, columns), BF16)
                    rl_ref[at, :] = jnp.zeros((part, columns), BF16)
                row = 0 if side == 0 else rows + 1
                status_ext_ref[pl.ds(row * c + y * part, part), :] = piece[4]
        for h in range(rows):
            at = pl.ds((h + 2) * c, c)
            ch_ref[at, :], cl_ref[at, :] = high_low(center_ref[h])
            rh_ref[at, :], rl_ref[at, :] = high_low(radius_ref[h])
            status_ext_ref[pl.ds((h + 1) * c, c), :] = status_ref[h].astype(F32).astype(BF16)
        pre_ref[pl.ds(0, c), :] = jnp.zeros((c, columns), BF16)
        pre_ref[pl.ds((rows + 1) * c, c), :] = jnp.zeros((c, columns), BF16)

        tall = jnp.broadcast_to(bias_ref[...], (8, c)).T[:, :1]
        tall = jnp.concatenate([tall, tall], axis=0)
        six = 6 * c

        @pl.loop(0, (rows + 2) // 2)
        def _(b):
            at = pl.ds(pl.multiple_of(b * 2 * c, 2 * c), 4 * c)
            here = pl.ds(pl.multiple_of(b * 2 * c, 2 * c), 2 * c)
            fh, fl, ah, al = (bands_ref[k * six : (k + 1) * six, :] for k in range(4))
            low = spread_columns(mul(fh, ch_ref[at, :]) + mul(fh, cl_ref[at, :]), columns)
            linear = low + tall
            center_out = linear + spread_columns(mul(fl, ch_ref[at, :]), columns)
            radius_out = spread_columns(
                mul(ah, rh_ref[at, :]) + mul(ah, rl_ref[at, :]) + mul(al, rh_ref[at, :]), columns
            )
            upper = center_out + radius_out
            lower = center_out - radius_out
            width = 2.0 * radius_out
            relaxed = jnp.minimum(jnp.maximum(upper, 0.0), width) / width
            status = status_ext_ref[here, :].astype(F32)
            open_ = status == 2.0
            slope = jnp.where(open_, relaxed, jnp.where(status == 1.0, 1.0, 0.0))
            slope_ref[here, :] = slope.astype(BF16)
            intercept = jnp.where(open_, -relaxed * jnp.minimum(lower, 0.0), 0.0)
            intercept_ref[here, :] = intercept.astype(BF16)
            linear_ref[here, :] = linear

        slope_edge_ref[0] = slope_ref[pl.ds(0, c), :]
        slope_edge_ref[1] = slope_ref[pl.ds((rows + 1) * c, c), :]

    total = jnp.zeros((8, columns), F32)
    for h in range(rows):
        at = pl.ds((h + 1) * c, c)
        coeff = coeff_ref[0, h]
        wide = coeff.astype(F32)
        pre = (wide * slope_ref[at, :].astype(F32)).astype(BF16)
        pre_ref[at, :] = pre
        terms = (
            jnp.minimum(wide, 0.0) * intercept_ref[at, :].astype(F32)
            + pre.astype(F32) * linear_ref[at, :]
        )
        total = total + jnp.sum(terms.reshape(c // 8, 8, columns), axis=0)

    for b in range(rows // 2):
        at = pl.ds(b * 2 * c, 4 * c)
        value = spread_columns(mul(bands_ref[24 * c :, :], pre_ref[at, :]), columns)
        for r in range(2):
            h = 2 * b + r
            row = value[r * c : (r + 1) * c]
            if h == 0 or h == rows - 1:
                edge_ref[0, 0 if h == 0 else 1] = row
            else:
                terms = jnp.abs(row) * radius_ref[h]
                total = total - jnp.sum(terms.reshape(c // 8, 8, columns), axis=0)
            out_ref[0, h] = row.astype(BF16)
    folded = total[:, :128]
    for k in range(1, columns // 128):
        folded = folded + total[:, k * 128 : (k + 1) * 128]
    total_ref[0] = folded


def main_pass(halo, center, radius, status, bands, bias, coeffs):
    specs, rows, channels, columns = coeffs.shape
    whole = lambda a: pl.BlockSpec(a.shape, lambda s, n=a.ndim: (0,) * n)
    ext = (rows + 4) * channels
    mid = (rows + 2) * channels
    return pl.pallas_call(
        main_kernel,
        grid=(specs,),
        out_shape=(
            jax.ShapeDtypeStruct(coeffs.shape, BF16),
            jax.ShapeDtypeStruct((specs, 2, channels, columns), F32),
            jax.ShapeDtypeStruct((2, channels, columns), BF16),
            jax.ShapeDtypeStruct((specs, 8, 128), F32),
        ),
        in_specs=[
            whole(a) for a in (halo, center, radius, status, bands, bias)
        ]
        + [pl.BlockSpec((1, rows, channels, columns), lambda s: (s, 0, 0, 0))],
        out_specs=(
            pl.BlockSpec((1, rows, channels, columns), lambda s: (s, 0, 0, 0)),
            pl.BlockSpec((1, 2, channels, columns), lambda s: (s, 0, 0, 0)),
            pl.BlockSpec((2, channels, columns), lambda s: (0, 0, 0)),
            pl.BlockSpec((1, 8, 128), lambda s: (s, 0, 0)),
        ),
        scratch_shapes=[pltpu.VMEM((ext, columns), BF16)] * 4
        + [
            pltpu.VMEM((mid, columns), BF16),
            pltpu.VMEM((mid, columns), BF16),
            pltpu.VMEM((mid, columns), BF16),
            pltpu.VMEM((mid, columns), F32),
            pltpu.VMEM((mid, columns), BF16),
        ],
        compiler_params=pltpu.CompilerParams(vmem_limit_bytes=MAIN_VMEM),
        cost_estimate=pl.CostEstimate(
            flops=MAIN_FLOPS, bytes_accessed=16 << 20, transcendentals=0
        ),
    )(halo, center, radius, status, bands, bias, coeffs)


def edge_kernel(
    one_ref,
    two_ref,
    slope_ref,
    edge_ref,
    radius_ref,
    weight_ref,
    total_ref,
    _,
    out_ref,
    sum_ref,
    halo_buf,
    edge_buf,
    slope_buf,
    radius_buf,
    weight_buf,
    done_ref,
    few_sems,
    sems,
):
    specs, channels, columns = one_ref.shape
    rows = out_ref.shape[1]
    odd = lax.rem(lax.axis_index("rows"), 2)
    which = (1 - odd, odd)
    copy = pltpu.make_async_copy
    few = [
        copy(slope_ref, slope_buf, few_sems.at[0]),
        copy(weight_ref, weight_buf, few_sems.at[1]),
        copy(radius_ref.at[0], radius_buf.at[0], few_sems.at[2]),
        copy(radius_ref.at[rows - 1], radius_buf.at[1], few_sems.at[3]),
    ]
    halos = [
        [copy(ref.at[s], halo_buf.at[k, s], sems.at[k, s]) for k, ref in enumerate((one_ref, two_ref))]
        for s in range(specs)
    ]
    edges = [copy(edge_ref.at[s], edge_buf.at[s], sems.at[2, s]) for s in range(specs)]
    stores = [
        [
            copy(done_ref.at[s, k], out_ref.at[s, which[k] * (rows - 1)], sems.at[3 + k, s])
            for k in range(2)
        ]
        for s in range(specs)
    ]
    for c in few:
        c.start()
    for s in range(specs):
        for c in (*halos[s], edges[s]):
            c.start()
    for c in few:
        c.wait()
    for s in range(specs):
        for c in (*halos[s], edges[s]):
            c.wait()
        total = total_ref[s]
        for k in range(2):
            e = which[k]
            pre = (halo_buf[k, s].astype(F32) * slope_buf[e].astype(F32)).astype(BF16)
            value = edge_buf[s, e] + spread_columns(mul(weight_buf[e], pre), columns)
            done_ref[s, k] = value.astype(BF16)
            stores[s][k].start()
            terms = jnp.abs(value) * radius_buf[e]
            terms = jnp.sum(terms.reshape(channels // 8, 8, columns), axis=0)
            for m in range(columns // 128):
                total = total - terms[:, m * 128 : (m + 1) * 128]
        sum_ref[s : s + 1, :] = jnp.sum(total, axis=0, keepdims=True)
    for s in range(specs):
        for c in stores[s]:
            c.wait()


def edge_pass(one, two, slope, edge, radius, weight, total, out):
    specs, rows, channels, columns = out.shape
    anywhere = pl.BlockSpec(memory_space=pl.ANY)
    inside = pl.BlockSpec(memory_space=pltpu.VMEM)
    return pl.pallas_call(
        edge_kernel,
        out_shape=(
            jax.ShapeDtypeStruct(out.shape, BF16),
            jax.ShapeDtypeStruct((specs, 128), F32),
        ),
        in_specs=[anywhere] * 6 + [inside, anywhere],
        out_specs=(anywhere, inside),
        scratch_shapes=[
            pltpu.VMEM((2, specs, channels, columns), BF16),
            pltpu.VMEM((specs, 2, channels, columns), F32),
            pltpu.VMEM((2, channels, columns), BF16),
            pltpu.VMEM((2, channels, columns), F32),
            pltpu.VMEM((2, 3 * channels, channels), BF16),
            pltpu.VMEM((specs, 2, channels, columns), BF16),
            pltpu.SemaphoreType.DMA((4,)),
            pltpu.SemaphoreType.DMA((5, specs)),
        ],
        input_output_aliases={7: 0},
        compiler_params=pltpu.CompilerParams(vmem_limit_bytes=EDGE_VMEM),
        cost_estimate=pl.CostEstimate(
            flops=EDGE_FLOPS, bytes_accessed=1 << 20, transcendentals=0
        ),
    )(one, two, slope, edge, radius, weight, total, out)


def weight_kernel(weight_ref, bands_ref, ends_ref):
    c = weight_ref.shape[2]
    zero = jnp.zeros((c, c), F32)

    def place(base, blocks):
        three = jnp.concatenate(blocks, axis=1)
        bands_ref[pl.ds(base, c), :] = jnp.concatenate([three, zero], axis=1).astype(BF16)
        bands_ref[pl.ds(base + c, c), :] = jnp.concatenate([zero, three], axis=1).astype(BF16)

    for j in range(3):
        turned = [weight_ref[i, j].T for i in range(3)]
        for base, blocks in ((0, turned), (12 * c, [jnp.abs(w) for w in turned])):
            high = [w.astype(BF16).astype(F32) for w in blocks]
            place(base + j * 2 * c, high)
            place(base + (3 + j) * 2 * c, [w - h for w, h in zip(blocks, high)])
        place((12 + j) * 2 * c, [weight_ref[i, 2 - j] for i in (2, 1, 0)])
        for k, i in enumerate((2, 0)):
            ends_ref[k, pl.ds(j * c, c), :] = weight_ref[i, 2 - j].astype(BF16)


def weight_pass(weight):
    c = weight.shape[2]
    whole = lambda a: pl.BlockSpec(a.shape, lambda g, n=len(a.shape): (0,) * n)
    out = (
        jax.ShapeDtypeStruct((30 * c, 4 * c), BF16),
        jax.ShapeDtypeStruct((2, 3 * c, c), BF16),
    )
    return pl.pallas_call(
        weight_kernel,
        grid=(1,),
        out_shape=out,
        in_specs=[whole(weight)],
        out_specs=tuple(whole(a) for a in out),
    )(weight)


def per_device(
    center, radius, conv_weight, conv_bias, split_status, out_coeffs, spec_ids, spec_offsets
):
    count, groups = (lax.axis_size("rows"), lax.axis_size("specs"))
    rows, columns, channels = center.shape
    center, radius, status = (jnp.swapaxes(a, 1, 2) for a in (center, radius, split_status))
    coeffs = jnp.swapaxes(out_coeffs, 2, 3)

    lanes = groups // SHARE
    mine, one, two = send_pass(lanes, center, radius, status, coeffs)
    moves = []
    for r in range(count):
        for s in range(groups):
            other = r + (1 if s % 2 == 0 else -1)
            if 0 <= other < count:
                moves.append((r * groups + s, other * groups + s))
    box = lax.ppermute(mine, ("rows", "specs"), moves)
    one, two = later_pass(one, two, mine)
    pairs = [(i, i + 1) for i in range(count - 1)]
    one = lax.ppermute(one, "rows", [m for p in pairs[::2] for m in (p, p[::-1])])
    two = lax.ppermute(two, "rows", [m for p in pairs[1::2] for m in (p, p[::-1])])
    halo = lax.all_gather(
        box,
        "specs",
        axis_index_groups=[
            [(k * lanes + z) * 2 + e for k in range(SHARE // 2) for e in range(2)]
            for z in range(lanes)
        ],
    )

    bands, ends = weight_pass(conv_weight)
    out, edge, slope, total = main_pass(
        halo, center, radius, status, bands, conv_bias[None, :], coeffs
    )
    out, partial = edge_pass(one, two, slope, edge, radius, ends, total, out)

    partial = partial + lax.ppermute(partial, "rows", [(i, i ^ 1) for i in range(count)])
    pairs = [partial] + [
        lax.ppermute(partial, "rows", [(i, i ^ step) for i in range(count)])
        for step in range(2, count, 2)
    ]
    while len(pairs) > 1:
        pairs = [a + b for a, b in zip(pairs[::2], pairs[1::2])]
    summed = jnp.sum(pairs[0], axis=1)
    pixels = rows * count * columns
    entries = spec_offsets.shape[0]
    onehot = spec_ids[:, None] == jnp.arange(entries, dtype=jnp.int32)[None, :]
    table_terms = jnp.sum(jnp.where(onehot, spec_offsets[None, :], 0.0), axis=1)
    bounds = summed / pixels + table_terms
    return (jnp.swapaxes(out, 2, 3), bounds)


def solution(mesh):
    in_specs = (
        P("rows", None, None),
        P("rows", None, None),
        P(),
        P(),
        P("rows", None, None),
        P("specs", "rows", None, None),
        P("specs"),
        P(),
    )
    out_specs = (P("specs", "rows", None, None), P("specs"))
    return jax.shard_map(
        per_device, mesh=mesh, in_specs=in_specs, out_specs=out_specs, check_vma=False
    )
```

```python
import functools

import functools

import jax
import jax.numpy as jnp
from jax import lax
from jax.experimental import pallas as pl
from jax.experimental.pallas import tpu as pltpu
from jax.sharding import PartitionSpec as P

F32, BF16 = (jnp.float32, jnp.bfloat16)
SHARE = 8
MAIN_FLOPS = 20_000_000_000
EDGE_FLOPS = 2_000_000_000
MAIN_VMEM = 44 << 20
EDGE_VMEM = 14 << 20
UNITS = 5


def spread_columns(stack, columns):
    size = stack.shape[0] // 3
    where = lax.broadcasted_iota(jnp.int32, (size, columns), 1)
    right = pltpu.roll(stack[:size], 1, 1)
    left = pltpu.roll(stack[2 * size :], columns - 1, 1)
    right = jnp.where(where == 0, 0.0, right)
    left = jnp.where(where == columns - 1, 0.0, left)
    return right + stack[size : 2 * size] + left


def mul(a, b):
    return jnp.dot(a, b, preferred_element_type=F32)


def high_low(value):
    high = value.astype(BF16)
    return high, (value - high.astype(F32)).astype(BF16)


def send_kernel(
    lanes,
    center_ref,
    radius_ref,
    status_ref,
    coeff_ref,
    box_ref,
    first_ref,
    second_ref,
    held_ref,
    center_box,
    radius_box,
    status_box,
    box_sems,
    sems,
):
    specs, rows = coeff_ref.shape[:2]
    part = box_ref.shape[1]
    me = lax.axis_index("specs")
    up = 1 - lax.rem(me, 2)
    here = pl.ds(pl.multiple_of(me // (2 * lanes) * part, part), part)
    two = pl.ds(up * (rows - 2), 2)
    one = pl.ds(up * (rows - 1), 1)
    odd = lax.rem(lax.axis_index("rows"), 2)
    boxes = [
        pltpu.make_async_copy(center_ref.at[two, here], center_box, box_sems.at[0]),
        pltpu.make_async_copy(radius_ref.at[two, here], radius_box, box_sems.at[1]),
        pltpu.make_async_copy(status_ref.at[one, here], status_box, box_sems.at[2]),
    ]
    todo = [
        (k, s, h * (rows - 1), ref)
        for k, (h, ref) in enumerate(((1 - odd, first_ref), (odd, second_ref)))
        for s in range(specs)
    ]
    reads = [
        pltpu.make_async_copy(coeff_ref.at[s, h], held_ref.at[k, s], sems.at[0, k, s])
        for k, s, h, _ in todo
    ]
    writes = [
        pltpu.make_async_copy(held_ref.at[k, s], ref.at[s], sems.at[1, k, s])
        for k, s, _, ref in todo
    ]
    for copy in boxes + reads:
        copy.start()
    for copy in boxes:
        copy.wait()
    box_ref[0:2] = center_box[...].astype(BF16)
    box_ref[2:4] = radius_box[...].astype(BF16)
    box_ref[4:5] = status_box[...].astype(F32).astype(BF16)
    for read, write in zip(reads, writes):
        read.wait()
        write.start()
    for write in writes:
        write.wait()


def send_pass(lanes, center, radius, status, coeffs):
    specs, rows, channels, columns = coeffs.shape
    part = channels * 2 // SHARE
    edge = jax.ShapeDtypeStruct((specs, channels, columns), BF16)
    anywhere = pl.BlockSpec(memory_space=pl.ANY)
    return pl.pallas_call(
        functools.partial(send_kernel, lanes),
        out_shape=(jax.ShapeDtypeStruct((UNITS, part, columns), BF16), edge, edge),
        in_specs=[anywhere] * 4,
        out_specs=(pl.BlockSpec(memory_space=pltpu.VMEM), anywhere, anywhere),
        scratch_shapes=[
            pltpu.VMEM((2, specs, channels, columns), BF16),
            pltpu.VMEM((2, part, columns), F32),
            pltpu.VMEM((2, part, columns), F32),
            pltpu.VMEM((1, part, columns), jnp.int32),
            pltpu.SemaphoreType.DMA((3,)),
            pltpu.SemaphoreType.DMA((2, 2, specs)),
        ],
        cost_estimate=pl.CostEstimate(flops=0, bytes_accessed=4 << 20, transcendentals=0),
    )(center, radius, status, coeffs)


def later_pass(first, second, box):
    def kernel(*refs):
        pass

    anywhere = pl.BlockSpec(memory_space=pl.ANY)
    return pl.pallas_call(
        kernel,
        out_shape=tuple(jax.ShapeDtypeStruct(a.shape, a.dtype) for a in (first, second)),
        in_specs=[anywhere] * 3,
        out_specs=(anywhere, anywhere),
        input_output_aliases={0: 0, 1: 1},
    )(first, second, box)


def main_kernel(
    halo_ref,
    center_ref,
    radius_ref,
    status_ref,
    bands_ref,
    bias_ref,
    coeff_ref,
    out_ref,
    edge_ref,
    slope_edge_ref,
    total_ref,
    ch_ref,
    cl_ref,
    rh_ref,
    rl_ref,
    status_ext_ref,
    slope_ref,
    intercept_ref,
    linear_ref,
    pre_ref,
):
    rows, channels, columns = center_ref.shape
    c = channels
    part = halo_ref.shape[2]

    @pl.when(pl.program_id(0) == 0)
    def _():
        for side, base in ((0, 0), (1, rows + 2)):
            for y in range(c // part):
                piece = halo_ref.at[2 * y + side]
                for k in range(2):
                    at = pl.ds((base + k) * c + y * part, part)
                    ch_ref[at, :] = piece[k]
                    rh_ref[at, :] = piece[2 + k]
                    cl_ref[at, :] = jnp.zeros((part, columns), BF16)
                    rl_ref[at, :] = jnp.zeros((part, columns), BF16)
                row = 0 if side == 0 else rows + 1
                status_ext_ref[pl.ds(row * c + y * part, part), :] = piece[4]
        for h in range(rows):
            at = pl.ds((h + 2) * c, c)
            ch_ref[at, :], cl_ref[at, :] = high_low(center_ref[h])
            rh_ref[at, :], rl_ref[at, :] = high_low(radius_ref[h])
            status_ext_ref[pl.ds((h + 1) * c, c), :] = status_ref[h].astype(F32).astype(BF16)
        pre_ref[pl.ds(0, c), :] = jnp.zeros((c, columns), BF16)
        pre_ref[pl.ds((rows + 1) * c, c), :] = jnp.zeros((c, columns), BF16)

        tall = jnp.broadcast_to(bias_ref[...], (8, c)).T[:, :1]
        tall = jnp.concatenate([tall, tall], axis=0)
        six = 6 * c

        @pl.loop(0, (rows + 2) // 2)
        def _(b):
            at = pl.ds(pl.multiple_of(b * 2 * c, 2 * c), 4 * c)
            here = pl.ds(pl.multiple_of(b * 2 * c, 2 * c), 2 * c)
            fh, fl, ah, al = (bands_ref[k * six : (k + 1) * six, :] for k in range(4))
            low = spread_columns(mul(fh, ch_ref[at, :]) + mul(fh, cl_ref[at, :]), columns)
            linear = low + tall
            center_out = linear + spread_columns(mul(fl, ch_ref[at, :]), columns)
            radius_out = spread_columns(
                mul(ah, rh_ref[at, :]) + mul(ah, rl_ref[at, :]) + mul(al, rh_ref[at, :]), columns
            )
            upper = center_out + radius_out
            lower = center_out - radius_out
            width = 2.0 * radius_out
            relaxed = jnp.minimum(jnp.maximum(upper, 0.0), width) / width
            status = status_ext_ref[here, :].astype(F32)
            open_ = status == 2.0
            slope = jnp.where(open_, relaxed, jnp.where(status == 1.0, 1.0, 0.0))
            slope_ref[here, :] = slope.astype(BF16)
            intercept = jnp.where(open_, -relaxed * jnp.minimum(lower, 0.0), 0.0)
            intercept_ref[here, :] = intercept.astype(BF16)
            linear_ref[here, :] = linear

        slope_edge_ref[0] = slope_ref[pl.ds(0, c), :]
        slope_edge_ref[1] = slope_ref[pl.ds((rows + 1) * c, c), :]

    total = jnp.zeros((8, columns), F32)
    for h in range(rows):
        at = pl.ds((h + 1) * c, c)
        coeff = coeff_ref[0, h]
        wide = coeff.astype(F32)
        pre = (wide * slope_ref[at, :].astype(F32)).astype(BF16)
        pre_ref[at, :] = pre
        terms = (
            jnp.minimum(wide, 0.0) * intercept_ref[at, :].astype(F32)
            + pre.astype(F32) * linear_ref[at, :]
        )
        total = total + jnp.sum(terms.reshape(c // 8, 8, columns), axis=0)

    for b in range(rows // 2):
        at = pl.ds(b * 2 * c, 4 * c)
        value = spread_columns(mul(bands_ref[24 * c :, :], pre_ref[at, :]), columns)
        for r in range(2):
            h = 2 * b + r
            row = value[r * c : (r + 1) * c]
            if h == 0 or h == rows - 1:
                edge_ref[0, 0 if h == 0 else 1] = row
            else:
                terms = jnp.abs(row) * radius_ref[h]
                total = total - jnp.sum(terms.reshape(c // 8, 8, columns), axis=0)
            out_ref[0, h] = row.astype(BF16)
    folded = total[:, :128]
    for k in range(1, columns // 128):
        folded = folded + total[:, k * 128 : (k + 1) * 128]
    total_ref[0] = folded


def main_pass(halo, center, radius, status, bands, bias, coeffs):
    specs, rows, channels, columns = coeffs.shape
    whole = lambda a: pl.BlockSpec(a.shape, lambda s, n=a.ndim: (0,) * n)
    ext = (rows + 4) * channels
    mid = (rows + 2) * channels
    return pl.pallas_call(
        main_kernel,
        grid=(specs,),
        out_shape=(
            jax.ShapeDtypeStruct(coeffs.shape, BF16),
            jax.ShapeDtypeStruct((specs, 2, channels, columns), F32),
            jax.ShapeDtypeStruct((2, channels, columns), BF16),
            jax.ShapeDtypeStruct((specs, 8, 128), F32),
        ),
        in_specs=[
            whole(a) for a in (halo, center, radius, status, bands, bias)
        ]
        + [pl.BlockSpec((1, rows, channels, columns), lambda s: (s, 0, 0, 0))],
        out_specs=(
            pl.BlockSpec((1, rows, channels, columns), lambda s: (s, 0, 0, 0)),
            pl.BlockSpec((1, 2, channels, columns), lambda s: (s, 0, 0, 0)),
            pl.BlockSpec((2, channels, columns), lambda s: (0, 0, 0)),
            pl.BlockSpec((1, 8, 128), lambda s: (s, 0, 0)),
        ),
        scratch_shapes=[pltpu.VMEM((ext, columns), BF16)] * 4
        + [
            pltpu.VMEM((mid, columns), BF16),
            pltpu.VMEM((mid, columns), BF16),
            pltpu.VMEM((mid, columns), BF16),
            pltpu.VMEM((mid, columns), F32),
            pltpu.VMEM((mid, columns), BF16),
        ],
        compiler_params=pltpu.CompilerParams(vmem_limit_bytes=MAIN_VMEM),
        cost_estimate=pl.CostEstimate(
            flops=MAIN_FLOPS, bytes_accessed=16 << 20, transcendentals=0
        ),
    )(halo, center, radius, status, bands, bias, coeffs)


def edge_kernel(
    sites_ref,
    one_ref,
    two_ref,
    slope_ref,
    edge_ref,
    radius_one_ref,
    radius_two_ref,
    weight_ref,
    total_ref,
    _,
    out_ref,
    sum_ref,
    done_ref,
    sems,
):
    specs, channels, columns = one_ref.shape
    rows = out_ref.shape[1]

    def store(s, k):
        row = sites_ref[k] * (rows - 1)
        return pltpu.make_async_copy(done_ref.at[s, k], out_ref.at[s, row], sems.at[s, k])

    for s in range(specs):
        total = total_ref[s]
        for k, (halo_ref, radius_ref) in enumerate(
            ((one_ref, radius_one_ref), (two_ref, radius_two_ref))
        ):
            e = sites_ref[k]
            pre = (halo_ref[s].astype(F32) * slope_ref[e].astype(F32)).astype(BF16)
            value = edge_ref[s, e] + spread_columns(mul(weight_ref[e], pre), columns)
            done_ref[s, k] = value.astype(BF16)
            terms = jnp.abs(value) * radius_ref[0]
            terms = jnp.sum(terms.reshape(channels // 8, 8, columns), axis=0)
            for m in range(columns // 128):
                total = total - terms[:, m * 128 : (m + 1) * 128]
        sum_ref[s : s + 1, :] = jnp.sum(total, axis=0, keepdims=True)
    for s in range(specs):
        for k in range(2):
            store(s, k).start()
    for s in range(specs):
        for k in range(2):
            store(s, k).wait()


def edge_pass(sites, one, two, slope, edge, radius, weight, total, out):
    specs, rows, channels, columns = out.shape
    whole = lambda a: pl.BlockSpec(a.shape, lambda g, e, n=a.ndim: (0,) * n)
    return pl.pallas_call(
        edge_kernel,
        out_shape=(
            jax.ShapeDtypeStruct(out.shape, BF16),
            jax.ShapeDtypeStruct((specs, 128), F32),
        ),
        grid_spec=pltpu.PrefetchScalarGridSpec(
            num_scalar_prefetch=1,
            grid=(1,),
            in_specs=[
                whole(one),
                whole(two),
                whole(slope),
                whole(edge),
                pl.BlockSpec((1, channels, columns), lambda g, e: (e[0] * (rows - 1), 0, 0)),
                pl.BlockSpec((1, channels, columns), lambda g, e: (e[1] * (rows - 1), 0, 0)),
                whole(weight),
                whole(total),
                pl.BlockSpec(memory_space=pl.ANY),
            ],
            out_specs=(
                pl.BlockSpec(memory_space=pl.ANY),
                pl.BlockSpec((specs, 128), lambda g, e: (0, 0)),
            ),
            scratch_shapes=[
                pltpu.VMEM((specs, 2, channels, columns), BF16),
                pltpu.SemaphoreType.DMA((specs, 2)),
            ],
        ),
        input_output_aliases={9: 0},
        compiler_params=pltpu.CompilerParams(vmem_limit_bytes=EDGE_VMEM),
        cost_estimate=pl.CostEstimate(
            flops=EDGE_FLOPS, bytes_accessed=1 << 20, transcendentals=0
        ),
    )(sites, one, two, slope, edge, radius, radius, weight, total, out)


def weight_kernel(weight_ref, bands_ref, ends_ref):
    c = weight_ref.shape[2]
    zero = jnp.zeros((c, c), F32)

    def place(base, blocks):
        three = jnp.concatenate(blocks, axis=1)
        bands_ref[pl.ds(base, c), :] = jnp.concatenate([three, zero], axis=1).astype(BF16)
        bands_ref[pl.ds(base + c, c), :] = jnp.concatenate([zero, three], axis=1).astype(BF16)

    for j in range(3):
        turned = [weight_ref[i, j].T for i in range(3)]
        for base, blocks in ((0, turned), (12 * c, [jnp.abs(w) for w in turned])):
            high = [w.astype(BF16).astype(F32) for w in blocks]
            place(base + j * 2 * c, high)
            place(base + (3 + j) * 2 * c, [w - h for w, h in zip(blocks, high)])
        place((12 + j) * 2 * c, [weight_ref[i, 2 - j] for i in (2, 1, 0)])
        for k, i in enumerate((2, 0)):
            ends_ref[k, pl.ds(j * c, c), :] = weight_ref[i, 2 - j].astype(BF16)


def weight_pass(weight):
    c = weight.shape[2]
    whole = lambda a: pl.BlockSpec(a.shape, lambda g, n=len(a.shape): (0,) * n)
    out = (
        jax.ShapeDtypeStruct((30 * c, 4 * c), BF16),
        jax.ShapeDtypeStruct((2, 3 * c, c), BF16),
    )
    return pl.pallas_call(
        weight_kernel,
        grid=(1,),
        out_shape=out,
        in_specs=[whole(weight)],
        out_specs=tuple(whole(a) for a in out),
    )(weight)


def per_device(
    center, radius, conv_weight, conv_bias, split_status, out_coeffs, spec_ids, spec_offsets
):
    count, groups = (lax.axis_size("rows"), lax.axis_size("specs"))
    rows, columns, channels = center.shape
    center, radius, status = (jnp.swapaxes(a, 1, 2) for a in (center, radius, split_status))
    coeffs = jnp.swapaxes(out_coeffs, 2, 3)

    lanes = groups // SHARE
    mine, one, two = send_pass(lanes, center, radius, status, coeffs)
    moves = []
    for r in range(count):
        for s in range(groups):
            other = r + (1 if s % 2 == 0 else -1)
            if 0 <= other < count:
                moves.append((r * groups + s, other * groups + s))
    box = lax.ppermute(mine, ("rows", "specs"), moves)
    one, two = later_pass(one, two, mine)
    pairs = [(i, i + 1) for i in range(count - 1)]
    one = lax.ppermute(one, "rows", [m for p in pairs[::2] for m in (p, p[::-1])])
    two = lax.ppermute(two, "rows", [m for p in pairs[1::2] for m in (p, p[::-1])])
    halo = lax.all_gather(
        box,
        "specs",
        axis_index_groups=[
            [(k * lanes + z) * 2 + e for k in range(SHARE // 2) for e in range(2)]
            for z in range(lanes)
        ],
    )

    bands, ends = weight_pass(conv_weight)
    out, edge, slope, total = main_pass(
        halo, center, radius, status, bands, conv_bias[None, :], coeffs
    )
    odd = lax.rem(lax.axis_index("rows"), 2)
    sites = jnp.stack([1 - odd, odd]).astype(jnp.int32)
    out, partial = edge_pass(sites, one, two, slope, edge, radius, ends, total, out)

    partial = partial + lax.ppermute(partial, "rows", [(i, i ^ 1) for i in range(count)])
    pairs = [partial] + [
        lax.ppermute(partial, "rows", [(i, i ^ step) for i in range(count)])
        for step in range(2, count, 2)
    ]
    while len(pairs) > 1:
        pairs = [a + b for a, b in zip(pairs[::2], pairs[1::2])]
    summed = jnp.sum(pairs[0], axis=1)
    pixels = rows * count * columns
    entries = spec_offsets.shape[0]
    onehot = spec_ids[:, None] == jnp.arange(entries, dtype=jnp.int32)[None, :]
    table_terms = jnp.sum(jnp.where(onehot, spec_offsets[None, :], 0.0), axis=1)
    bounds = summed / pixels + table_terms
    return (jnp.swapaxes(out, 2, 3), bounds)


def solution(mesh):
    in_specs = (
        P("rows", None, None),
        P("rows", None, None),
        P(),
        P(),
        P("rows", None, None),
        P("specs", "rows", None, None),
        P("specs"),
        P(),
    )
    out_specs = (P("specs", "rows", None, None), P("specs"))
    return jax.shard_map(
        per_device, mesh=mesh, in_specs=in_specs, out_specs=out_specs, check_vma=False
    )
```

```python
import functools

import functools

import jax
import jax.numpy as jnp
from jax import lax
from jax.experimental import pallas as pl
from jax.experimental.pallas import tpu as pltpu
from jax.sharding import PartitionSpec as P

F32, BF16 = (jnp.float32, jnp.bfloat16)
SHARE = 8
MAIN_FLOPS = 20_000_000_000
EDGE_FLOPS = 2_000_000_000
MAIN_VMEM = 44 << 20
EDGE_VMEM = 14 << 20
UNITS = 5


def spread_columns(stack, columns):
    size = stack.shape[0] // 3
    where = lax.broadcasted_iota(jnp.int32, (size, columns), 1)
    right = pltpu.roll(stack[:size], 1, 1)
    left = pltpu.roll(stack[2 * size :], columns - 1, 1)
    right = jnp.where(where == 0, 0.0, right)
    left = jnp.where(where == columns - 1, 0.0, left)
    return right + stack[size : 2 * size] + left


def mul(a, b):
    return jnp.dot(a, b, preferred_element_type=F32)


def high_low(value):
    high = value.astype(BF16)
    return high, (value - high.astype(F32)).astype(BF16)


def payload_kernel(
    lanes, center_ref, radius_ref, status_ref, box_ref, center_box, radius_box, status_box, sems
):
    rows = center_ref.shape[0]
    part = box_ref.shape[1]
    me = lax.axis_index("specs")
    up = 1 - lax.rem(me, 2)
    here = pl.ds(pl.multiple_of(me // (2 * lanes) * part, part), part)
    two = pl.ds(up * (rows - 2), 2)
    one = pl.ds(up * (rows - 1), 1)
    copies = [
        pltpu.make_async_copy(center_ref.at[two, here], center_box, sems.at[0]),
        pltpu.make_async_copy(radius_ref.at[two, here], radius_box, sems.at[1]),
        pltpu.make_async_copy(status_ref.at[one, here], status_box, sems.at[2]),
    ]
    for copy in copies:
        copy.start()
    for copy in copies:
        copy.wait()
    box_ref[0:2] = center_box[...].astype(BF16)
    box_ref[2:4] = radius_box[...].astype(BF16)
    box_ref[4:5] = status_box[...].astype(F32).astype(BF16)


def payload_pass(lanes, center, radius, status):
    rows, channels, columns = center.shape
    part = channels * 2 // SHARE
    return pl.pallas_call(
        functools.partial(payload_kernel, lanes),
        out_shape=jax.ShapeDtypeStruct((UNITS, part, columns), BF16),
        in_specs=[pl.BlockSpec(memory_space=pl.ANY)] * 3,
        out_specs=pl.BlockSpec(memory_space=pltpu.VMEM),
        scratch_shapes=[
            pltpu.VMEM((2, part, columns), F32),
            pltpu.VMEM((2, part, columns), F32),
            pltpu.VMEM((1, part, columns), jnp.int32),
            pltpu.SemaphoreType.DMA((3,)),
        ],
        cost_estimate=pl.CostEstimate(flops=0, bytes_accessed=1 << 20, transcendentals=0),
    )(center, radius, status)


def send_kernel(coeff_ref, _, first_ref, second_ref, held_ref, sems):
    specs, rows = coeff_ref.shape[:2]
    odd = lax.rem(lax.axis_index("rows"), 2)
    todo = [
        (k, s, h * (rows - 1), ref)
        for k, (h, ref) in enumerate(((1 - odd, first_ref), (odd, second_ref)))
        for s in range(specs)
    ]
    reads = [
        pltpu.make_async_copy(coeff_ref.at[s, h], held_ref.at[k, s], sems.at[0, k, s])
        for k, s, h, _ in todo
    ]
    writes = [
        pltpu.make_async_copy(held_ref.at[k, s], ref.at[s], sems.at[1, k, s])
        for k, s, _, ref in todo
    ]
    for read in reads:
        read.start()
    for read, write in zip(reads, writes):
        read.wait()
        write.start()
    for write in writes:
        write.wait()


def send_pass(coeffs, after):
    specs, rows, channels, columns = coeffs.shape
    edge = jax.ShapeDtypeStruct((specs, channels, columns), BF16)
    anywhere = pl.BlockSpec(memory_space=pl.ANY)
    return pl.pallas_call(
        send_kernel,
        out_shape=(edge, edge),
        in_specs=[anywhere, anywhere],
        out_specs=(anywhere, anywhere),
        scratch_shapes=[
            pltpu.VMEM((2, specs, channels, columns), BF16),
            pltpu.SemaphoreType.DMA((2, 2, specs)),
        ],
        cost_estimate=pl.CostEstimate(flops=0, bytes_accessed=4 << 20, transcendentals=0),
    )(coeffs, after)


def main_kernel(
    halo_ref,
    center_ref,
    radius_ref,
    status_ref,
    bands_ref,
    bias_ref,
    coeff_ref,
    out_ref,
    edge_ref,
    slope_edge_ref,
    total_ref,
    ch_ref,
    cl_ref,
    rh_ref,
    rl_ref,
    status_ext_ref,
    slope_ref,
    intercept_ref,
    linear_ref,
    pre_ref,
):
    rows, channels, columns = center_ref.shape
    c = channels
    part = halo_ref.shape[2]

    @pl.when(pl.program_id(0) == 0)
    def _():
        for side, base in ((0, 0), (1, rows + 2)):
            for y in range(c // part):
                piece = halo_ref.at[2 * y + side]
                for k in range(2):
                    at = pl.ds((base + k) * c + y * part, part)
                    ch_ref[at, :] = piece[k]
                    rh_ref[at, :] = piece[2 + k]
                    cl_ref[at, :] = jnp.zeros((part, columns), BF16)
                    rl_ref[at, :] = jnp.zeros((part, columns), BF16)
                row = 0 if side == 0 else rows + 1
                status_ext_ref[pl.ds(row * c + y * part, part), :] = piece[4]
        for h in range(rows):
            at = pl.ds((h + 2) * c, c)
            ch_ref[at, :], cl_ref[at, :] = high_low(center_ref[h])
            rh_ref[at, :], rl_ref[at, :] = high_low(radius_ref[h])
            status_ext_ref[pl.ds((h + 1) * c, c), :] = status_ref[h].astype(F32).astype(BF16)
        pre_ref[pl.ds(0, c), :] = jnp.zeros((c, columns), BF16)
        pre_ref[pl.ds((rows + 1) * c, c), :] = jnp.zeros((c, columns), BF16)

        tall = jnp.broadcast_to(bias_ref[...], (8, c)).T[:, :1]
        tall = jnp.concatenate([tall, tall], axis=0)
        six = 6 * c

        @pl.loop(0, (rows + 2) // 2)
        def _(b):
            at = pl.ds(pl.multiple_of(b * 2 * c, 2 * c), 4 * c)
            here = pl.ds(pl.multiple_of(b * 2 * c, 2 * c), 2 * c)
            fh, fl, ah, al = (bands_ref[k * six : (k + 1) * six, :] for k in range(4))
            low = spread_columns(mul(fh, ch_ref[at, :]) + mul(fh, cl_ref[at, :]), columns)
            linear = low + tall
            center_out = linear + spread_columns(mul(fl, ch_ref[at, :]), columns)
            radius_out = spread_columns(
                mul(ah, rh_ref[at, :]) + mul(ah, rl_ref[at, :]) + mul(al, rh_ref[at, :]), columns
            )
            upper = center_out + radius_out
            lower = center_out - radius_out
            width = 2.0 * radius_out
            relaxed = jnp.minimum(jnp.maximum(upper, 0.0), width) / width
            status = status_ext_ref[here, :].astype(F32)
            open_ = status == 2.0
            slope = jnp.where(open_, relaxed, jnp.where(status == 1.0, 1.0, 0.0))
            slope_ref[here, :] = slope.astype(BF16)
            intercept = jnp.where(open_, -relaxed * jnp.minimum(lower, 0.0), 0.0)
            intercept_ref[here, :] = intercept.astype(BF16)
            linear_ref[here, :] = linear

        slope_edge_ref[0] = slope_ref[pl.ds(0, c), :]
        slope_edge_ref[1] = slope_ref[pl.ds((rows + 1) * c, c), :]

    total = jnp.zeros((8, columns), F32)
    for h in range(rows):
        at = pl.ds((h + 1) * c, c)
        coeff = coeff_ref[0, h]
        wide = coeff.astype(F32)
        pre = (wide * slope_ref[at, :].astype(F32)).astype(BF16)
        pre_ref[at, :] = pre
        terms = (
            jnp.minimum(wide, 0.0) * intercept_ref[at, :].astype(F32)
            + pre.astype(F32) * linear_ref[at, :]
        )
        total = total + jnp.sum(terms.reshape(c // 8, 8, columns), axis=0)

    for b in range(rows // 2):
        at = pl.ds(b * 2 * c, 4 * c)
        value = spread_columns(mul(bands_ref[24 * c :, :], pre_ref[at, :]), columns)
        for r in range(2):
            h = 2 * b + r
            row = value[r * c : (r + 1) * c]
            if h == 0 or h == rows - 1:
                edge_ref[0, 0 if h == 0 else 1] = row
            else:
                terms = jnp.abs(row) * radius_ref[h]
                total = total - jnp.sum(terms.reshape(c // 8, 8, columns), axis=0)
            out_ref[0, h] = row.astype(BF16)
    folded = total[:, :128]
    for k in range(1, columns // 128):
        folded = folded + total[:, k * 128 : (k + 1) * 128]
    total_ref[0] = folded


def main_pass(halo, center, radius, status, bands, bias, coeffs):
    specs, rows, channels, columns = coeffs.shape
    whole = lambda a: pl.BlockSpec(a.shape, lambda s, n=a.ndim: (0,) * n)
    ext = (rows + 4) * channels
    mid = (rows + 2) * channels
    return pl.pallas_call(
        main_kernel,
        grid=(specs,),
        out_shape=(
            jax.ShapeDtypeStruct(coeffs.shape, BF16),
            jax.ShapeDtypeStruct((specs, 2, channels, columns), F32),
            jax.ShapeDtypeStruct((2, channels, columns), BF16),
            jax.ShapeDtypeStruct((specs, 8, 128), F32),
        ),
        in_specs=[
            whole(a) for a in (halo, center, radius, status, bands, bias)
        ]
        + [pl.BlockSpec((1, rows, channels, columns), lambda s: (s, 0, 0, 0))],
        out_specs=(
            pl.BlockSpec((1, rows, channels, columns), lambda s: (s, 0, 0, 0)),
            pl.BlockSpec((1, 2, channels, columns), lambda s: (s, 0, 0, 0)),
            pl.BlockSpec((2, channels, columns), lambda s: (0, 0, 0)),
            pl.BlockSpec((1, 8, 128), lambda s: (s, 0, 0)),
        ),
        scratch_shapes=[pltpu.VMEM((ext, columns), BF16)] * 4
        + [
            pltpu.VMEM((mid, columns), BF16),
            pltpu.VMEM((mid, columns), BF16),
            pltpu.VMEM((mid, columns), BF16),
            pltpu.VMEM((mid, columns), F32),
            pltpu.VMEM((mid, columns), BF16),
        ],
        compiler_params=pltpu.CompilerParams(vmem_limit_bytes=MAIN_VMEM),
        cost_estimate=pl.CostEstimate(
            flops=MAIN_FLOPS, bytes_accessed=16 << 20, transcendentals=0
        ),
    )(halo, center, radius, status, bands, bias, coeffs)


def edge_kernel(
    sites_ref,
    one_ref,
    two_ref,
    slope_ref,
    edge_ref,
    radius_one_ref,
    radius_two_ref,
    weight_ref,
    total_ref,
    done_ref,
    sum_ref,
):
    specs, channels, columns = one_ref.shape
    for s in range(specs):
        total = total_ref[s]
        for k, (halo_ref, radius_ref) in enumerate(
            ((one_ref, radius_one_ref), (two_ref, radius_two_ref))
        ):
            e = sites_ref[k]
            pre = (halo_ref[s].astype(F32) * slope_ref[e].astype(F32)).astype(BF16)
            value = edge_ref[s, e] + spread_columns(mul(weight_ref[e], pre), columns)
            done_ref[s, k] = value.astype(BF16)
            terms = jnp.abs(value) * radius_ref[0]
            terms = jnp.sum(terms.reshape(channels // 8, 8, columns), axis=0)
            for m in range(columns // 128):
                total = total - terms[:, m * 128 : (m + 1) * 128]
        sum_ref[s : s + 1, :] = jnp.sum(total, axis=0, keepdims=True)


def edge_pass(sites, one, two, slope, edge, radius, weight, total):
    specs, channels, columns = one.shape
    rows = radius.shape[0]
    whole = lambda a: pl.BlockSpec(a.shape, lambda g, e, n=len(a.shape): (0,) * n)
    out = (
        jax.ShapeDtypeStruct((specs, 2, channels, columns), BF16),
        jax.ShapeDtypeStruct((specs, 128), F32),
    )
    return pl.pallas_call(
        edge_kernel,
        out_shape=out,
        grid_spec=pltpu.PrefetchScalarGridSpec(
            num_scalar_prefetch=1,
            grid=(1,),
            in_specs=[
                whole(one),
                whole(two),
                whole(slope),
                whole(edge),
                pl.BlockSpec((1, channels, columns), lambda g, e: (e[0] * (rows - 1), 0, 0)),
                pl.BlockSpec((1, channels, columns), lambda g, e: (e[1] * (rows - 1), 0, 0)),
                whole(weight),
                whole(total),
            ],
            out_specs=tuple(whole(a) for a in out),
        ),
        compiler_params=pltpu.CompilerParams(vmem_limit_bytes=EDGE_VMEM),
        cost_estimate=pl.CostEstimate(
            flops=EDGE_FLOPS, bytes_accessed=1 << 20, transcendentals=0
        ),
    )(sites, one, two, slope, edge, radius, radius, weight, total)


def place_kernel(sites_ref, done_ref, _, out_ref, sems):
    specs = done_ref.shape[0]
    rows = out_ref.shape[1]
    copies = [
        pltpu.make_async_copy(
            done_ref.at[s, k], out_ref.at[s, sites_ref[k] * (rows - 1)], sems.at[s, k]
        )
        for s in range(specs)
        for k in range(2)
    ]
    for copy in copies:
        copy.start()
    for copy in copies:
        copy.wait()


def place_pass(sites, done, out):
    anywhere = pl.BlockSpec(memory_space=pl.ANY)
    return pl.pallas_call(
        place_kernel,
        out_shape=jax.ShapeDtypeStruct(out.shape, BF16),
        grid_spec=pltpu.PrefetchScalarGridSpec(
            num_scalar_prefetch=1,
            grid=(1,),
            in_specs=[pl.BlockSpec(done.shape, lambda g, e: (0, 0, 0, 0)), anywhere],
            out_specs=anywhere,
            scratch_shapes=[pltpu.SemaphoreType.DMA(done.shape[:2])],
        ),
        input_output_aliases={2: 0},
        compiler_params=pltpu.CompilerParams(vmem_limit_bytes=16 << 20),
        cost_estimate=pl.CostEstimate(flops=0, bytes_accessed=4 << 20, transcendentals=0),
    )(sites, done, out)


def weight_kernel(weight_ref, bands_ref, ends_ref):
    c = weight_ref.shape[2]
    zero = jnp.zeros((c, c), F32)

    def place(base, blocks):
        three = jnp.concatenate(blocks, axis=1)
        bands_ref[pl.ds(base, c), :] = jnp.concatenate([three, zero], axis=1).astype(BF16)
        bands_ref[pl.ds(base + c, c), :] = jnp.concatenate([zero, three], axis=1).astype(BF16)

    for j in range(3):
        turned = [weight_ref[i, j].T for i in range(3)]
        for base, blocks in ((0, turned), (12 * c, [jnp.abs(w) for w in turned])):
            high = [w.astype(BF16).astype(F32) for w in blocks]
            place(base + j * 2 * c, high)
            place(base + (3 + j) * 2 * c, [w - h for w, h in zip(blocks, high)])
        place((12 + j) * 2 * c, [weight_ref[i, 2 - j] for i in (2, 1, 0)])
        for k, i in enumerate((2, 0)):
            ends_ref[k, pl.ds(j * c, c), :] = weight_ref[i, 2 - j].astype(BF16)


def weight_pass(weight):
    c = weight.shape[2]
    whole = lambda a: pl.BlockSpec(a.shape, lambda g, n=len(a.shape): (0,) * n)
    out = (
        jax.ShapeDtypeStruct((30 * c, 4 * c), BF16),
        jax.ShapeDtypeStruct((2, 3 * c, c), BF16),
    )
    return pl.pallas_call(
        weight_kernel,
        grid=(1,),
        out_shape=out,
        in_specs=[whole(weight)],
        out_specs=tuple(whole(a) for a in out),
    )(weight)


def per_device(
    center, radius, conv_weight, conv_bias, split_status, out_coeffs, spec_ids, spec_offsets
):
    count, groups = (lax.axis_size("rows"), lax.axis_size("specs"))
    rows, columns, channels = center.shape
    center, radius, status = (jnp.swapaxes(a, 1, 2) for a in (center, radius, split_status))
    coeffs = jnp.swapaxes(out_coeffs, 2, 3)

    lanes = groups // SHARE
    mine = payload_pass(lanes, center, radius, status)
    center, radius, status, mine = lax.optimization_barrier((center, radius, status, mine))
    moves = []
    for r in range(count):
        for s in range(groups):
            other = r + (1 if s % 2 == 0 else -1)
            if 0 <= other < count:
                moves.append((r * groups + s, other * groups + s))
    box = lax.ppermute(mine, ("rows", "specs"), moves)
    one, two = send_pass(coeffs, mine)
    pairs = [(i, i + 1) for i in range(count - 1)]
    one = lax.ppermute(one, "rows", [m for p in pairs[::2] for m in (p, p[::-1])])
    two = lax.ppermute(two, "rows", [m for p in pairs[1::2] for m in (p, p[::-1])])
    halo = lax.all_gather(
        box,
        "specs",
        axis_index_groups=[
            [(k * lanes + z) * 2 + e for k in range(SHARE // 2) for e in range(2)]
            for z in range(lanes)
        ],
    )

    bands, ends = weight_pass(conv_weight)
    out, edge, slope, total = main_pass(
        halo, center, radius, status, bands, conv_bias[None, :], coeffs
    )
    odd = lax.rem(lax.axis_index("rows"), 2)
    sites = jnp.stack([1 - odd, odd]).astype(jnp.int32)
    done, partial = edge_pass(sites, one, two, slope, edge, radius, ends, total)
    out = place_pass(sites, done, out)

    partial = partial + lax.ppermute(partial, "rows", [(i, i ^ 1) for i in range(count)])
    pairs = [partial] + [
        lax.ppermute(partial, "rows", [(i, i ^ step) for i in range(count)])
        for step in range(2, count, 2)
    ]
    while len(pairs) > 1:
        pairs = [a + b for a, b in zip(pairs[::2], pairs[1::2])]
    summed = jnp.sum(pairs[0], axis=1)
    pixels = rows * count * columns
    entries = spec_offsets.shape[0]
    onehot = spec_ids[:, None] == jnp.arange(entries, dtype=jnp.int32)[None, :]
    table_terms = jnp.sum(jnp.where(onehot, spec_offsets[None, :], 0.0), axis=1)
    bounds = summed / pixels + table_terms
    return (jnp.swapaxes(out, 2, 3), bounds)


def solution(mesh):
    in_specs = (
        P("rows", None, None),
        P("rows", None, None),
        P(),
        P(),
        P("rows", None, None),
        P("specs", "rows", None, None),
        P("specs"),
        P(),
    )
    out_specs = (P("specs", "rows", None, None), P("specs"))
    return jax.shard_map(
        per_device, mesh=mesh, in_specs=in_specs, out_specs=out_specs, check_vma=False
    )
```

```python
import functools

import functools

import jax
import jax.numpy as jnp
from jax import lax
from jax.experimental import pallas as pl
from jax.experimental.pallas import tpu as pltpu
from jax.sharding import PartitionSpec as P

F32, BF16 = (jnp.float32, jnp.bfloat16)
SHARE = 8
MAIN_FLOPS = 2_000_000_000
EDGE_FLOPS = 10_000_000_000
MAIN_VMEM = 44 << 20
EDGE_VMEM = 14 << 20
UNITS = 5


def spread_columns(stack, columns):
    size = stack.shape[0] // 3
    where = lax.broadcasted_iota(jnp.int32, (size, columns), 1)
    right = pltpu.roll(stack[:size], 1, 1)
    left = pltpu.roll(stack[2 * size :], columns - 1, 1)
    right = jnp.where(where == 0, 0.0, right)
    left = jnp.where(where == columns - 1, 0.0, left)
    return right + stack[size : 2 * size] + left


def mul(a, b):
    return jnp.dot(a, b, preferred_element_type=F32)


def high_low(value):
    high = value.astype(BF16)
    return high, (value - high.astype(F32)).astype(BF16)


def payload_kernel(
    lanes, center_ref, radius_ref, status_ref, box_ref, center_box, radius_box, status_box, sems
):
    rows = center_ref.shape[0]
    part = box_ref.shape[1]
    me = lax.axis_index("specs")
    up = 1 - lax.rem(me, 2)
    here = pl.ds(pl.multiple_of(me // (2 * lanes) * part, part), part)
    two = pl.ds(up * (rows - 2), 2)
    one = pl.ds(up * (rows - 1), 1)
    copies = [
        pltpu.make_async_copy(center_ref.at[two, here], center_box, sems.at[0]),
        pltpu.make_async_copy(radius_ref.at[two, here], radius_box, sems.at[1]),
        pltpu.make_async_copy(status_ref.at[one, here], status_box, sems.at[2]),
    ]
    for copy in copies:
        copy.start()
    for copy in copies:
        copy.wait()
    box_ref[0:2] = center_box[...].astype(BF16)
    box_ref[2:4] = radius_box[...].astype(BF16)
    box_ref[4:5] = status_box[...].astype(F32).astype(BF16)


def payload_pass(lanes, center, radius, status):
    rows, channels, columns = center.shape
    part = channels * 2 // SHARE
    return pl.pallas_call(
        functools.partial(payload_kernel, lanes),
        out_shape=jax.ShapeDtypeStruct((UNITS, part, columns), BF16),
        in_specs=[pl.BlockSpec(memory_space=pl.ANY)] * 3,
        out_specs=pl.BlockSpec(memory_space=pltpu.VMEM),
        scratch_shapes=[
            pltpu.VMEM((2, part, columns), F32),
            pltpu.VMEM((2, part, columns), F32),
            pltpu.VMEM((1, part, columns), jnp.int32),
            pltpu.SemaphoreType.DMA((3,)),
        ],
        cost_estimate=pl.CostEstimate(flops=0, bytes_accessed=1 << 20, transcendentals=0),
    )(center, radius, status)


def send_kernel(coeff_ref, _, first_ref, second_ref, held_ref, sems):
    specs, rows = coeff_ref.shape[:2]
    odd = lax.rem(lax.axis_index("rows"), 2)
    todo = [
        (k, s, h * (rows - 1), ref)
        for k, (h, ref) in enumerate(((1 - odd, first_ref), (odd, second_ref)))
        for s in range(specs)
    ]
    reads = [
        pltpu.make_async_copy(coeff_ref.at[s, h], held_ref.at[k, s], sems.at[0, k, s])
        for k, s, h, _ in todo
    ]
    writes = [
        pltpu.make_async_copy(held_ref.at[k, s], ref.at[s], sems.at[1, k, s])
        for k, s, _, ref in todo
    ]
    for read in reads:
        read.start()
    for read, write in zip(reads, writes):
        read.wait()
        write.start()
    for write in writes:
        write.wait()


def send_pass(coeffs, after):
    specs, rows, channels, columns = coeffs.shape
    edge = jax.ShapeDtypeStruct((specs, channels, columns), BF16)
    anywhere = pl.BlockSpec(memory_space=pl.ANY)
    return pl.pallas_call(
        send_kernel,
        out_shape=(edge, edge),
        in_specs=[anywhere, anywhere],
        out_specs=(anywhere, anywhere),
        scratch_shapes=[
            pltpu.VMEM((2, specs, channels, columns), BF16),
            pltpu.SemaphoreType.DMA((2, 2, specs)),
        ],
        cost_estimate=pl.CostEstimate(flops=0, bytes_accessed=4 << 20, transcendentals=0),
    )(coeffs, after)


def main_kernel(
    halo_ref,
    center_ref,
    radius_ref,
    status_ref,
    bands_ref,
    bias_ref,
    coeff_ref,
    out_ref,
    edge_ref,
    slope_edge_ref,
    total_ref,
    ch_ref,
    cl_ref,
    rh_ref,
    rl_ref,
    status_ext_ref,
    slope_ref,
    intercept_ref,
    linear_ref,
    pre_ref,
):
    rows, channels, columns = center_ref.shape
    c = channels
    part = halo_ref.shape[2]

    @pl.when(pl.program_id(0) == 0)
    def _():
        for side, base in ((0, 0), (1, rows + 2)):
            for y in range(c // part):
                piece = halo_ref.at[2 * y + side]
                for k in range(2):
                    at = pl.ds((base + k) * c + y * part, part)
                    ch_ref[at, :] = piece[k]
                    rh_ref[at, :] = piece[2 + k]
                    cl_ref[at, :] = jnp.zeros((part, columns), BF16)
                    rl_ref[at, :] = jnp.zeros((part, columns), BF16)
                row = 0 if side == 0 else rows + 1
                status_ext_ref[pl.ds(row * c + y * part, part), :] = piece[4]
        for h in range(rows):
            at = pl.ds((h + 2) * c, c)
            ch_ref[at, :], cl_ref[at, :] = high_low(center_ref[h])
            rh_ref[at, :], rl_ref[at, :] = high_low(radius_ref[h])
            status_ext_ref[pl.ds((h + 1) * c, c), :] = status_ref[h].astype(F32).astype(BF16)
        pre_ref[pl.ds(0, c), :] = jnp.zeros((c, columns), BF16)
        pre_ref[pl.ds((rows + 1) * c, c), :] = jnp.zeros((c, columns), BF16)

        tall = jnp.broadcast_to(bias_ref[...], (8, c)).T[:, :1]
        tall = jnp.concatenate([tall, tall], axis=0)
        six = 6 * c

        @pl.loop(0, (rows + 2) // 2)
        def _(b):
            at = pl.ds(pl.multiple_of(b * 2 * c, 2 * c), 4 * c)
            here = pl.ds(pl.multiple_of(b * 2 * c, 2 * c), 2 * c)
            fh, fl, ah, al = (bands_ref[k * six : (k + 1) * six, :] for k in range(4))
            low = spread_columns(mul(fh, ch_ref[at, :]) + mul(fh, cl_ref[at, :]), columns)
            linear = low + tall
            center_out = linear + spread_columns(mul(fl, ch_ref[at, :]), columns)
            radius_out = spread_columns(
                mul(ah, rh_ref[at, :]) + mul(ah, rl_ref[at, :]) + mul(al, rh_ref[at, :]), columns
            )
            upper = center_out + radius_out
            lower = center_out - radius_out
            width = 2.0 * radius_out
            relaxed = jnp.minimum(jnp.maximum(upper, 0.0), width) / width
            status = status_ext_ref[here, :].astype(F32)
            open_ = status == 2.0
            slope = jnp.where(open_, relaxed, jnp.where(status == 1.0, 1.0, 0.0))
            slope_ref[here, :] = slope.astype(BF16)
            intercept = jnp.where(open_, -relaxed * jnp.minimum(lower, 0.0), 0.0)
            intercept_ref[here, :] = intercept.astype(BF16)
            linear_ref[here, :] = linear

        slope_edge_ref[0] = slope_ref[pl.ds(0, c), :]
        slope_edge_ref[1] = slope_ref[pl.ds((rows + 1) * c, c), :]

    total = jnp.zeros((8, columns), F32)
    for h in range(rows):
        at = pl.ds((h + 1) * c, c)
        coeff = coeff_ref[0, h]
        wide = coeff.astype(F32)
        pre = (wide * slope_ref[at, :].astype(F32)).astype(BF16)
        pre_ref[at, :] = pre
        terms = (
            jnp.minimum(wide, 0.0) * intercept_ref[at, :].astype(F32)
            + pre.astype(F32) * linear_ref[at, :]
        )
        total = total + jnp.sum(terms.reshape(c // 8, 8, columns), axis=0)

    for b in range(rows // 2):
        at = pl.ds(b * 2 * c, 4 * c)
        value = spread_columns(mul(bands_ref[24 * c :, :], pre_ref[at, :]), columns)
        for r in range(2):
            h = 2 * b + r
            row = value[r * c : (r + 1) * c]
            if h == 0 or h == rows - 1:
                edge_ref[0, 0 if h == 0 else 1] = row
            else:
                terms = jnp.abs(row) * radius_ref[h]
                total = total - jnp.sum(terms.reshape(c // 8, 8, columns), axis=0)
            out_ref[0, h] = row.astype(BF16)
    folded = total[:, :128]
    for k in range(1, columns // 128):
        folded = folded + total[:, k * 128 : (k + 1) * 128]
    total_ref[0] = folded


def main_pass(halo, center, radius, status, bands, bias, coeffs):
    specs, rows, channels, columns = coeffs.shape
    whole = lambda a: pl.BlockSpec(a.shape, lambda s, n=a.ndim: (0,) * n)
    ext = (rows + 4) * channels
    mid = (rows + 2) * channels
    return pl.pallas_call(
        main_kernel,
        grid=(specs,),
        out_shape=(
            jax.ShapeDtypeStruct(coeffs.shape, BF16),
            jax.ShapeDtypeStruct((specs, 2, channels, columns), F32),
            jax.ShapeDtypeStruct((2, channels, columns), BF16),
            jax.ShapeDtypeStruct((specs, 8, 128), F32),
        ),
        in_specs=[
            whole(a) for a in (halo, center, radius, status, bands, bias)
        ]
        + [pl.BlockSpec((1, rows, channels, columns), lambda s: (s, 0, 0, 0))],
        out_specs=(
            pl.BlockSpec((1, rows, channels, columns), lambda s: (s, 0, 0, 0)),
            pl.BlockSpec((1, 2, channels, columns), lambda s: (s, 0, 0, 0)),
            pl.BlockSpec((2, channels, columns), lambda s: (0, 0, 0)),
            pl.BlockSpec((1, 8, 128), lambda s: (s, 0, 0)),
        ),
        scratch_shapes=[pltpu.VMEM((ext, columns), BF16)] * 4
        + [
            pltpu.VMEM((mid, columns), BF16),
            pltpu.VMEM((mid, columns), BF16),
            pltpu.VMEM((mid, columns), BF16),
            pltpu.VMEM((mid, columns), F32),
            pltpu.VMEM((mid, columns), BF16),
        ],
        compiler_params=pltpu.CompilerParams(vmem_limit_bytes=MAIN_VMEM),
        cost_estimate=pl.CostEstimate(
            flops=MAIN_FLOPS, bytes_accessed=16 << 20, transcendentals=0
        ),
    )(halo, center, radius, status, bands, bias, coeffs)


def edge_kernel(
    last, sites_ref, halo_ref, slope_ref, edge_ref, radius_ref, weight_ref, total_ref, done_ref, sum_ref
):
    specs, channels, columns = halo_ref.shape
    for s in range(specs):
        pre = (halo_ref[s].astype(F32) * slope_ref[0].astype(F32)).astype(BF16)
        value = edge_ref[s, 0] + spread_columns(mul(weight_ref[0], pre), columns)
        done_ref[s] = value.astype(BF16)
        terms = jnp.abs(value) * radius_ref[0]
        terms = jnp.sum(terms.reshape(channels // 8, 8, columns), axis=0)
        total = total_ref[s]
        for m in range(columns // 128):
            total = total - terms[:, m * 128 : (m + 1) * 128]
        if last:
            sum_ref[s : s + 1, :] = jnp.sum(total, axis=0, keepdims=True)
        else:
            sum_ref[s] = total


def edge_pass(k, sites, halo, slope, edge, radius, weight, total):
    specs, channels, columns = halo.shape
    rows = radius.shape[0]
    whole = lambda a: pl.BlockSpec(a.shape, lambda g, e, n=len(a.shape): (0,) * n)
    last = k == 1
    out = (
        jax.ShapeDtypeStruct((specs, channels, columns), BF16),
        jax.ShapeDtypeStruct((specs, 128) if last else total.shape, F32),
    )
    return pl.pallas_call(
        functools.partial(edge_kernel, last),
        out_shape=out,
        grid_spec=pltpu.PrefetchScalarGridSpec(
            num_scalar_prefetch=1,
            grid=(1,),
            in_specs=[
                whole(halo),
                pl.BlockSpec((1, channels, columns), lambda g, e: (e[k], 0, 0)),
                pl.BlockSpec((specs, 1, channels, columns), lambda g, e: (0, e[k], 0, 0)),
                pl.BlockSpec((1, channels, columns), lambda g, e: (e[k] * (rows - 1), 0, 0)),
                pl.BlockSpec((1, 3 * channels, channels), lambda g, e: (e[k], 0, 0)),
                whole(total),
            ],
            out_specs=tuple(whole(a) for a in out),
        ),
        compiler_params=pltpu.CompilerParams(vmem_limit_bytes=EDGE_VMEM),
        cost_estimate=pl.CostEstimate(
            flops=EDGE_FLOPS, bytes_accessed=1 << 20, transcendentals=0
        ),
    )(sites, halo, slope, edge, radius, weight, total)


def place_kernel(sites_ref, one_ref, two_ref, _, out_ref, sems):
    specs = one_ref.shape[0]
    rows = out_ref.shape[1]
    copies = [
        pltpu.make_async_copy(
            ref.at[s], out_ref.at[s, sites_ref[k] * (rows - 1)], sems.at[s, k]
        )
        for s in range(specs)
        for k, ref in enumerate((one_ref, two_ref))
    ]
    for copy in copies:
        copy.start()
    for copy in copies:
        copy.wait()


def place_pass(sites, one, two, out):
    anywhere = pl.BlockSpec(memory_space=pl.ANY)
    return pl.pallas_call(
        place_kernel,
        out_shape=jax.ShapeDtypeStruct(out.shape, BF16),
        grid_spec=pltpu.PrefetchScalarGridSpec(
            num_scalar_prefetch=1,
            grid=(1,),
            in_specs=[pl.BlockSpec(one.shape, lambda g, e: (0, 0, 0))] * 2 + [anywhere],
            out_specs=anywhere,
            scratch_shapes=[pltpu.SemaphoreType.DMA((one.shape[0], 2))],
        ),
        input_output_aliases={3: 0},
        compiler_params=pltpu.CompilerParams(vmem_limit_bytes=16 << 20),
        cost_estimate=pl.CostEstimate(flops=0, bytes_accessed=4 << 20, transcendentals=0),
    )(sites, one, two, out)


def weight_kernel(weight_ref, bands_ref, ends_ref):
    c = weight_ref.shape[2]
    zero = jnp.zeros((c, c), F32)

    def place(base, blocks):
        three = jnp.concatenate(blocks, axis=1)
        bands_ref[pl.ds(base, c), :] = jnp.concatenate([three, zero], axis=1).astype(BF16)
        bands_ref[pl.ds(base + c, c), :] = jnp.concatenate([zero, three], axis=1).astype(BF16)

    for j in range(3):
        turned = [weight_ref[i, j].T for i in range(3)]
        for base, blocks in ((0, turned), (12 * c, [jnp.abs(w) for w in turned])):
            high = [w.astype(BF16).astype(F32) for w in blocks]
            place(base + j * 2 * c, high)
            place(base + (3 + j) * 2 * c, [w - h for w, h in zip(blocks, high)])
        place((12 + j) * 2 * c, [weight_ref[i, 2 - j] for i in (2, 1, 0)])
        for k, i in enumerate((2, 0)):
            ends_ref[k, pl.ds(j * c, c), :] = weight_ref[i, 2 - j].astype(BF16)


def weight_pass(weight):
    c = weight.shape[2]
    whole = lambda a: pl.BlockSpec(a.shape, lambda g, n=len(a.shape): (0,) * n)
    out = (
        jax.ShapeDtypeStruct((30 * c, 4 * c), BF16),
        jax.ShapeDtypeStruct((2, 3 * c, c), BF16),
    )
    return pl.pallas_call(
        weight_kernel,
        grid=(1,),
        out_shape=out,
        in_specs=[whole(weight)],
        out_specs=tuple(whole(a) for a in out),
    )(weight)


def per_device(
    center, radius, conv_weight, conv_bias, split_status, out_coeffs, spec_ids, spec_offsets
):
    count, groups = (lax.axis_size("rows"), lax.axis_size("specs"))
    rows, columns, channels = center.shape
    center, radius, status = (jnp.swapaxes(a, 1, 2) for a in (center, radius, split_status))
    coeffs = jnp.swapaxes(out_coeffs, 2, 3)

    lanes = groups // SHARE
    mine = payload_pass(lanes, center, radius, status)
    center, radius, status, mine = lax.optimization_barrier((center, radius, status, mine))
    moves = []
    for r in range(count):
        for s in range(groups):
            other = r + (1 if s % 2 == 0 else -1)
            if 0 <= other < count:
                moves.append((r * groups + s, other * groups + s))
    box = lax.ppermute(mine, ("rows", "specs"), moves)
    one, two = send_pass(coeffs, mine)
    pairs = [(i, i + 1) for i in range(count - 1)]
    one = lax.ppermute(one, "rows", [m for p in pairs[::2] for m in (p, p[::-1])])
    two = lax.ppermute(two, "rows", [m for p in pairs[1::2] for m in (p, p[::-1])])
    halo = lax.all_gather(
        box,
        "specs",
        axis_index_groups=[
            [(k * lanes + z) * 2 + e for k in range(SHARE // 2) for e in range(2)]
            for z in range(lanes)
        ],
    )

    bands, ends = weight_pass(conv_weight)
    out, edge, slope, total = main_pass(
        halo, center, radius, status, bands, conv_bias[None, :], coeffs
    )
    odd = lax.rem(lax.axis_index("rows"), 2)
    sites = jnp.stack([1 - odd, odd]).astype(jnp.int32)
    one, total = edge_pass(0, sites, one, slope, edge, radius, ends, total)
    two, partial = edge_pass(1, sites, two, slope, edge, radius, ends, total)
    out = place_pass(sites, one, two, out)

    partial = partial + lax.ppermute(partial, "rows", [(i, i ^ 1) for i in range(count)])
    pairs = [partial] + [
        lax.ppermute(partial, "rows", [(i, i ^ step) for i in range(count)])
        for step in range(2, count, 2)
    ]
    while len(pairs) > 1:
        pairs = [a + b for a, b in zip(pairs[::2], pairs[1::2])]
    summed = jnp.sum(pairs[0], axis=1)
    pixels = rows * count * columns
    entries = spec_offsets.shape[0]
    onehot = spec_ids[:, None] == jnp.arange(entries, dtype=jnp.int32)[None, :]
    table_terms = jnp.sum(jnp.where(onehot, spec_offsets[None, :], 0.0), axis=1)
    bounds = summed / pixels + table_terms
    return (jnp.swapaxes(out, 2, 3), bounds)


def solution(mesh):
    in_specs = (
        P("rows", None, None),
        P("rows", None, None),
        P(),
        P(),
        P("rows", None, None),
        P("specs", "rows", None, None),
        P("specs"),
        P(),
    )
    out_specs = (P("specs", "rows", None, None), P("specs"))
    return jax.shard_map(
        per_device, mesh=mesh, in_specs=in_specs, out_specs=out_specs, check_vma=False
    )
```
